32 devices in a mesh: blk: 8 (over z, x), grp: 4 (over y, core).
Axes of the slice: x: 2, y: 2, z: 4, core: 2. Of those that a mesh axis runs over, the one named last changes fastest.
Arguments:
- flow: float32 [384, 5, 4096], P(('blk', 'grp')), may hold values from -3 to 6, as said below
- adjoint: float32 [384, 5, 4096], P(('blk', 'grp')), may hold values from -6 to 6
- cut_flag: int32 [384, 4096], P(('blk', 'grp')), may hold values 0 or 1
- lateral_owner: int32 [384, 4, 1], P(('blk', 'grp')), may hold values from 0 to 7; in each aligned block of 48 rows (0 to 47, 48 to 95, ..., all dimensions but the last counted through in order) at most 9 rows name the same one
- lateral_link: int32 [384, 4], P(('blk', 'grp')), may hold values from 0 to 59
- vertical_link: int32 [384, 2], P(('blk', 'grp')), may hold values from 0 to 59
Outputs:
- indicator: float32 [384, 4096], P(('blk', 'grp'))
The draws below stay inside these ranges and needn't reach their ends.
Inputs may be any that keep to these rules, and one draw needn't show every extreme that they name: `flow`: density lies between 1 and 2, pressure between 1 and 2, every velocity component between -1.25 and 1.25. `lateral_owner`: among the faces 0 to 3 of the blocks of one device, at most 9 have their neighbour on any one blk index, and in every draw some device reaches 9.
All inputs are finite; a program needn't handle non-finite values. No bound on the sum of `cut_flag` on one device may be relied on, other than what follows from the above.
Results may differ from the reference program's by a relative error of at most 0.0003.
Values sent between devices are 32-bit elements; how exact they have to be, the bound alone decides.
A program may use at most 128 MiB of HBM per device.

```python
import math
import jax
import jax.numpy as jnp
import numpy as np
from jax import lax

EDGE = 16
BLK_DEV = 12
CELLS = 4096
NB = 384
CAP = 9
N_BLK = 8
N_GRP = 4


def draw_flow(key, part):
    keys = jax.random.split(key, 9)
    grid_shape = (NB, CELLS)
    density = jnp.exp(jax.random.uniform(keys[0], grid_shape, jnp.float32, 0.0, math.log(2.0)))
    pressure = jnp.exp(jax.random.uniform(keys[1], grid_shape, jnp.float32, 0.0, math.log(2.0)))
    velocity = jnp.clip(0.25 * jax.random.normal(keys[2], (3,) + grid_shape, jnp.float32), -0.5, 0.5)
    transonic = jax.random.uniform(keys[3], (NB, 1), jnp.float32) < 0.125
    direction = jax.random.randint(keys[4], (NB, 1), 0, 3)
    heading = jnp.where(jax.random.uniform(keys[5], (NB, 1), jnp.float32) < 0.5, -1.0, 1.0)
    magnitude = jax.random.uniform(keys[6], grid_shape, jnp.float32, 0.75, 1.25)
    fast_density = jax.random.uniform(keys[7], grid_shape, jnp.float32, 1.6, 2.0)
    fast_pressure = jax.random.uniform(keys[8], grid_shape, jnp.float32, 1.0, 1.2)
    density = jnp.where(transonic, fast_density, density)
    pressure = jnp.where(transonic, fast_pressure, pressure)
    component = jnp.arange(3, dtype=jnp.int32)[:, None, None]
    picked = (component == direction[None]) & transonic[None]
    velocity = jnp.where(picked, (heading * magnitude)[None], velocity)
    energy = pressure / 0.4 + 0.5 * density * jnp.sum(velocity * velocity, axis=0)
    return jnp.stack([density, density * velocity[0], density * velocity[1], density * velocity[2], energy], axis=1)


def plant(drawn, rng, low, top_value):
    extent = drawn.shape
    spot = [jax.random.randint(jax.random.fold_in(rng, axis), (), 0, extent[axis]) for axis in range(len(extent))]
    drawn = drawn.at[tuple(spot)].set(low)
    longest = extent.index(max(extent))
    spot[longest] = (spot[longest] + 1) % extent[longest]
    return drawn.at[tuple(spot)].set(top_value)


def level_of(rng, shape, cuts, low, high):
    gain = 1.0
    for axis_at, blocks in cuts:
        steps = jax.random.uniform(jax.random.fold_in(jax.random.fold_in(rng, 6), axis_at), (blocks,), jnp.float32, low / len(cuts), high / len(cuts))
        gain = gain * jnp.repeat(jnp.exp(steps), shape[axis_at] // blocks).reshape((-1,) + (1,) * (len(shape) - 1 - axis_at))
    return gain


def assign_block(key, own, number, rows, number_of, top, reach, slope):
    order = jax.random.permutation(key, number_of)
    heavy_load, common = shares(number_of, rows * top, reach, slope, True), shares(number_of, rows * top, reach, slope, False)
    places = jnp.arange(number_of)

    def named(tallies, offset_by):
        used = int((tallies > 0).sum())
        fixed = max(1, used // 4)
        moved = fixed + (places - fixed + offset_by * (used - fixed)) % max(1, number_of - fixed)
        return jnp.zeros((number_of,), jnp.int32).at[order[jnp.where(places < fixed, places, moved)]].set(jnp.asarray(tallies, jnp.int32))

    tallies = jnp.where(number % 4 == 0, named(heavy_load, number // 4), named(common, number - number // 4 - 1))
    mixed = jax.random.permutation(jax.random.fold_in(own, 3), number_of)
    giver, sink = mixed[0:number_of // 2 * 2:2], mixed[1:number_of // 2 * 2:2]
    slack = jnp.minimum(tallies[giver] - 1, reach - tallies[sink]) // 2
    slack = jnp.where((giver == order[0]) | (sink == order[0]) | (tallies[sink] == 0), 0, jnp.maximum(slack, 0))
    moved = jax.random.randint(jax.random.fold_in(own, 4), (number_of // 2,), 0, 1 << 20) % (slack + 1)
    tallies = tallies.at[giver].add(-moved).at[sink].add(moved)
    labels = jnp.searchsorted(jnp.cumsum(tallies), jnp.arange(rows * top), side="right").astype(jnp.int32)
    table = labels.reshape(top, rows).T
    table = table[jax.random.permutation(jax.random.fold_in(own, 1), rows)]
    offset_by = jax.random.randint(jax.random.fold_in(own, 2), (rows, 1), 0, top)
    return jnp.take_along_axis(table, (jnp.arange(top)[None, :] + offset_by) % top, axis=1)


def shares(count, total, limit, lean, full):
    weights = [(1 << 20) // math.isqrt(standing ** lean) + 1 for standing in range(1, count + 1)]
    largest = limit if full else min(limit, max(-(-total // count), total * weights[0] // sum(weights)))
    least = 1 if total - largest >= count - 1 else 0
    holding, rest = [largest] + [least] * (count - 1), total - largest - least * (count - 1)
    while rest > 0:
        movable = [i for i in range(1, count) if holding[i] < largest] or [i for i in range(1, count) if holding[i] < limit]
        whole, budget = sum([weights[i] for i in movable]), rest
        for i in movable:
            addition = min(limit - holding[i], max(1, budget * weights[i] // whole), rest)
            holding[i] = holding[i] + addition
            rest = rest - addition
    return np.array(holding)


def centred(rng, dims, scale, bound, shards=(), held_as=jnp.bfloat16):
    loudness = level_of(rng, dims, shards, -0.22, 0.18) if shards else 1.0
    values = jax.random.normal(rng, dims, jnp.float32) * scale * loudness
    return jnp.minimum(jnp.maximum(values, -bound), bound).astype(held_as)


def setup_inputs(seed: int = 0) -> dict:
    splits = jax.random.split(jax.random.key(seed), 7)
    flow = draw_flow(jax.random.fold_in(splits[6], 71), 0)
    adjoint = centred(splits[1], (NB, 5, CELLS), 1.0, 6.0, ((0, 32),), jnp.float32)
    cut_flag = plant((jax.random.randint(splits[2], (NB, CELLS), 0, 8) < 1).astype(jnp.int32), jax.random.fold_in(splits[2], 1), 0, 1)
    lateral_owner_keys = jax.random.split(jax.random.fold_in(splits[3], 1), NB * 4 // (4 * BLK_DEV))
    lateral_owner_turns = jax.random.permutation(jax.random.fold_in(splits[3], 3), NB * 4 // (4 * BLK_DEV))
    lateral_owner = jax.vmap(lambda own, number: assign_block(jax.random.fold_in(splits[3], 2), own, number, 4 * BLK_DEV, N_BLK, 1, CAP, 2))(lateral_owner_keys, lateral_owner_turns).reshape((NB, 4, 1))
    lateral_link = plant(jax.random.randint(splits[4], (NB, 4), 0, 5 * BLK_DEV), jax.random.fold_in(splits[4], 1), 0, (5 * BLK_DEV) - 1).astype(jnp.int32)
    vertical_link = plant(jax.random.randint(splits[5], (NB, 2), 0, 5 * BLK_DEV), jax.random.fold_in(splits[5], 1), 0, (5 * BLK_DEV) - 1).astype(jnp.int32)
    return {"flow": flow, "adjoint": adjoint, "cut_flag": cut_flag, "lateral_owner": lateral_owner, "lateral_link": lateral_link, "vertical_link": vertical_link}


HEAT_RATIO = 1.4
ENTROPY_FIX = 0.2
FREESTREAM = (1.0, 0.0, 0.0, 0.3, 1.0)

def primitive(conserved):
    density = conserved[:, 0]
    velocity = conserved[:, 1:4] / density[:, None]
    pressure = (HEAT_RATIO - 1.0) * (conserved[:, 4] - 0.5 * density * lax.optimization_barrier(jnp.sum(velocity * velocity, axis=1)))
    return jnp.concatenate([density[:, None], velocity, pressure[:, None]], axis=1)

def minmod(first_diff, second_diff):
    return jnp.where(first_diff * second_diff > 0.0, jnp.sign(first_diff) * jnp.minimum(jnp.abs(first_diff), jnp.abs(second_diff)), 0.0)

def harten(wave_rate, spread):
    return jnp.where(wave_rate < spread, (wave_rate * wave_rate + spread * spread) / (2.0 * spread), wave_rate)

def roe_flux(left_state, right_state, normal_axis):
    left_rho = left_state[0]
    right_rho = right_state[0]
    left_vel = left_state[1:4]
    right_vel = right_state[1:4]
    left_press = left_state[4]
    right_press = right_state[4]
    factor = HEAT_RATIO / (HEAT_RATIO - 1.0)
    left_enth = factor * left_press / left_rho + 0.5 * lax.optimization_barrier(jnp.sum(left_vel * left_vel, axis=0))
    right_enth = factor * right_press / right_rho + 0.5 * lax.optimization_barrier(jnp.sum(right_vel * right_vel, axis=0))
    left_root = jnp.sqrt(left_rho)
    right_root = jnp.sqrt(right_rho)
    weight_sum = left_root + right_root
    mean_vel = (left_root * left_vel + right_root * right_vel) / weight_sum
    mean_enth = (left_root * left_enth + right_root * right_enth) / weight_sum
    speed_sq = lax.optimization_barrier(jnp.sum(mean_vel * mean_vel, axis=0))
    sound_sq = (HEAT_RATIO - 1.0) * (mean_enth - 0.5 * speed_sq)
    sound_speed = jnp.sqrt(sound_sq)
    mean_rho = left_root * right_root
    normal = mean_vel[normal_axis]
    jump_vel = right_vel - left_vel
    jump_rho = right_rho - left_rho
    jump_press = right_press - left_press
    jump_normal = jump_vel[normal_axis]
    wave_slow = (jump_press - mean_rho * sound_speed * jump_normal) / (2.0 * sound_sq)
    wave_fast = (jump_press + mean_rho * sound_speed * jump_normal) / (2.0 * sound_sq)
    wave_entropy = jump_rho - jump_press / sound_sq
    spread = ENTROPY_FIX * sound_speed
    slow_part = harten(jnp.abs(normal - sound_speed), spread) * wave_slow
    fast_part = harten(jnp.abs(normal + sound_speed), spread) * wave_fast
    mid_part = jnp.abs(normal) * wave_entropy
    shear_part = jnp.abs(normal) * mean_rho
    unit_vector = [1.0 if axis_no == normal_axis else 0.0 for axis_no in range(3)]
    shear_jump = [jump_vel[axis_no] - jump_normal * unit_vector[axis_no] for axis_no in range(3)]
    diss_mass = slow_part + fast_part + mid_part
    diss_mom = [slow_part * (mean_vel[axis_no] - sound_speed * unit_vector[axis_no]) + fast_part * (mean_vel[axis_no] + sound_speed * unit_vector[axis_no]) + mid_part * mean_vel[axis_no] + shear_part * shear_jump[axis_no] for axis_no in range(3)]
    diss_energy = slow_part * (mean_enth - normal * sound_speed) + fast_part * (mean_enth + normal * sound_speed) + mid_part * 0.5 * speed_sq + shear_part * (mean_vel[0] * shear_jump[0] + mean_vel[1] * shear_jump[1] + mean_vel[2] * shear_jump[2])
    left_normal = left_vel[normal_axis]
    right_normal = right_vel[normal_axis]
    mass_flux = 0.5 * (left_rho * left_normal + right_rho * right_normal) - 0.5 * diss_mass
    momentum = [0.5 * (left_rho * left_normal * left_vel[axis_no] + right_rho * right_normal * right_vel[axis_no] + (left_press + right_press) * unit_vector[axis_no]) - 0.5 * diss_mom[axis_no] for axis_no in range(3)]
    energy = 0.5 * (left_rho * left_normal * left_enth + right_rho * right_normal * right_enth) - 0.5 * diss_energy
    return jnp.stack([mass_flux] + momentum + [energy], axis=0)

def wall_flux(pressure, normal_axis):
    nothing = jnp.zeros_like(pressure)
    parts = [pressure if axis_no == normal_axis else nothing for axis_no in range(3)]
    return jnp.stack([nothing] + parts + [nothing], axis=0)

def face_flux(left_state, right_state, left_solid, right_solid, normal_axis):
    roe_value = roe_flux(left_state, right_state, normal_axis)
    from_left = (right_solid > 0.5) & (left_solid < 0.5)
    from_right = (left_solid > 0.5) & (right_solid < 0.5)
    return jnp.where(from_left, wall_flux(left_state[4], normal_axis), jnp.where(from_right, wall_flux(right_state[4], normal_axis), roe_value))

def faces_of(coarse_cube):
    face_shape = (coarse_cube.shape[0], coarse_cube.shape[1], EDGE * EDGE)
    return jnp.stack([coarse_cube[:, :, 0].reshape(face_shape), coarse_cube[:, :, -1].reshape(face_shape), coarse_cube[:, :, :, 0].reshape(face_shape), coarse_cube[:, :, :, -1].reshape(face_shape), coarse_cube[:, :, :, :, 0].reshape(face_shape), coarse_cube[:, :, :, :, -1].reshape(face_shape)], axis=1)

def select_face(face_slab, level_code):
    channels = face_slab.shape[0]
    half_edge = EDGE // 2
    square = face_slab.reshape(channels, EDGE, EDGE)
    quarter_code = jnp.minimum(level_code, 3)
    anchor = jnp.zeros((), jnp.int32)
    first_start = (quarter_code // 2 * half_edge).astype(jnp.int32)
    second_start = (quarter_code % 2 * half_edge).astype(jnp.int32)
    quarter = lax.dynamic_slice(square, (anchor, first_start, second_start), (channels, half_edge, half_edge))
    widened = jnp.broadcast_to(quarter[:, :, None, :, None], (channels, half_edge, 2, half_edge, 2))
    return jnp.where(level_code == 4, face_slab, widened.reshape(channels, EDGE * EDGE))

def prolong(coarse_cube, ghosts):
    channels = coarse_cube.shape[0]
    edge_cells = coarse_cube.shape[1]
    slopes = []
    for axis_no in range(3):
        dim_no = axis_no + 1
        lower_side = jnp.concatenate([jnp.expand_dims(ghosts[2 * axis_no], dim_no), lax.slice_in_dim(coarse_cube, 0, edge_cells - 1, axis=dim_no)], axis=dim_no)
        upper_side = jnp.concatenate([lax.slice_in_dim(coarse_cube, 1, edge_cells, axis=dim_no), jnp.expand_dims(ghosts[2 * axis_no + 1], dim_no)], axis=dim_no)
        slopes.append(minmod(upper_side - coarse_cube, coarse_cube - lower_side))
    split_shape = (channels, edge_cells, 1, edge_cells, 1, edge_cells, 1)
    child_signs = jnp.array([-0.25, 0.25], jnp.float32)
    fine_field = coarse_cube.reshape(split_shape) + slopes[0].reshape(split_shape) * child_signs[:, None, None, None, None] + slopes[1].reshape(split_shape) * child_signs[:, None, None] + slopes[2].reshape(split_shape) * child_signs
    return fine_field.reshape(channels, 2 * edge_cells, 2 * edge_cells, 2 * edge_cells)

def residual(fine_field, fine_ghosts, solid_mask):
    size_fine = fine_field.shape[1]
    summed = jnp.zeros_like(fine_field)
    for axis_no in range(3):
        dim_no = axis_no + 1
        left_state = jnp.concatenate([jnp.expand_dims(fine_ghosts[2 * axis_no], dim_no), fine_field], axis=dim_no)
        right_state = jnp.concatenate([fine_field, jnp.expand_dims(fine_ghosts[2 * axis_no + 1], dim_no)], axis=dim_no)
        open_rim = jnp.expand_dims(jnp.zeros((size_fine, size_fine), jnp.float32), axis_no)
        left_solid = jnp.concatenate([open_rim, solid_mask], axis=axis_no)
        right_solid = jnp.concatenate([solid_mask, open_rim], axis=axis_no)
        flux_all = face_flux(left_state, right_state, left_solid, right_solid, axis_no)
        summed = summed + lax.slice_in_dim(flux_all, 1, size_fine + 1, axis=dim_no) - lax.slice_in_dim(flux_all, 0, size_fine, axis=dim_no)
    return jnp.where(solid_mask[None] > 0.5, 0.0, summed)

def block_indicator(operands):
    flow_prim, adjoint_block, ghosts, flags = operands
    coarse_flow = flow_prim.reshape(5, EDGE, EDGE, EDGE)
    coarse_adjoint = adjoint_block.reshape(5, EDGE, EDGE, EDGE)
    face_ghosts = ghosts.reshape(6, 10, EDGE, EDGE)
    fine_flow = prolong(coarse_flow, face_ghosts[:, :5])
    fine_adjoint = prolong(coarse_adjoint, face_ghosts[:, 5:])
    wide_ghosts = jnp.broadcast_to(face_ghosts[:, :5, :, None, :, None], (6, 5, EDGE, 2, EDGE, 2)).reshape(6, 5, 2 * EDGE, 2 * EDGE)
    solid_mask = jnp.broadcast_to(flags.astype(jnp.float32).reshape(EDGE, 1, EDGE, 1, EDGE, 1), (EDGE, 2, EDGE, 2, EDGE, 2)).reshape(2 * EDGE, 2 * EDGE, 2 * EDGE)
    fine_residual = residual(fine_flow, wide_ghosts, solid_mask)
    weighted = lax.optimization_barrier(jnp.sum(fine_adjoint * fine_residual, axis=0))
    coarse = weighted.reshape(EDGE, 2, EDGE, 2, EDGE, 2).sum(axis=(1, 3, 5))
    return jnp.abs(coarse).reshape(EDGE * EDGE * EDGE)

def reference(flow, adjoint, cut_flag, lateral_owner, lateral_link, vertical_link):
    number_blocks = flow.shape[0]
    primitives = primitive(flow)
    coarse_both = jnp.concatenate([primitives, adjoint], axis=1).reshape(number_blocks, 10, EDGE, EDGE, EDGE)
    face_all = faces_of(coarse_both)
    block_ids = jnp.arange(number_blocks, dtype=jnp.int32)
    device_ids = block_ids // BLK_DEV
    region = device_ids % N_GRP
    column = device_ids // N_GRP
    lateral_block = (lateral_owner[:, :, 0] * N_GRP + region[:, None]) * BLK_DEV + lateral_link // 5
    opposite = jnp.array([1, 0, 3, 2], jnp.int32)
    lateral_slab = face_all[lateral_block, opposite[None, :]]
    lateral_ghost = jax.vmap(jax.vmap(select_face))(lateral_slab, lateral_link % 5)
    lower_region = jnp.maximum(region - 1, 0)
    upper_region = jnp.minimum(region + 1, N_GRP - 1)
    lower_block = (column * N_GRP + lower_region) * BLK_DEV + vertical_link[:, 0] // 5
    upper_block = (column * N_GRP + upper_region) * BLK_DEV + vertical_link[:, 1] // 5
    lower_ghost = jax.vmap(select_face)(face_all[lower_block, 5], vertical_link[:, 0] % 5)
    upper_ghost = jax.vmap(select_face)(face_all[upper_block, 4], vertical_link[:, 1] % 5)
    state = jnp.array(FREESTREAM, jnp.float32)
    farfield_layer = jnp.concatenate([jnp.broadcast_to(state[:, None], (5, EDGE * EDGE)), jnp.zeros((5, EDGE * EDGE), jnp.float32)], axis=0)
    lower_ghost = jnp.where((region == 0)[:, None, None], farfield_layer, lower_ghost)
    upper_ghost = jnp.where((region == N_GRP - 1)[:, None, None], farfield_layer, upper_ghost)
    ghosts = jnp.concatenate([lateral_ghost, lower_ghost[:, None], upper_ghost[:, None]], axis=1)
    return lax.map(block_indicator, (primitives, adjoint, ghosts, cut_flag))
```

```python
import functools

import jax
import jax.numpy as jnp
from jax import lax
from jax.experimental import pallas as pl
from jax.experimental.pallas import tpu as pltpu
from jax.sharding import PartitionSpec as P

EDGE = 16
PLANE = EDGE * EDGE
LANES = 128
PACK = 4
FREESTREAM = (1.0, 0.0, 0.0, 0.3, 1.0)
VMEM = pl.BlockSpec(memory_space=pltpu.VMEM)
SMEM = pl.BlockSpec(memory_space=pltpu.SMEM)
HBM = pl.BlockSpec(memory_space=pltpu.HBM)
MESH = pl.DeviceIdType.MESH


def iota(shape, dim):
    return lax.broadcasted_iota(jnp.int32, shape, dim)


def primitive(state):
    density, mom, energy = state[0], state[1:4], state[4]
    root = lax.rsqrt(density)
    inverse = root * root
    vel = [m * inverse for m in mom]
    square = vel[0] * vel[0] + vel[1] * vel[1] + vel[2] * vel[2]
    return [density, *vel, 0.4 * (energy - 0.5 * density * square)]


def pack_cells(flow_ref, adj_ref, flag_ref, val_ref, solid_ref):
    blocks = flow_ref.shape[1]
    groups = blocks // PACK
    top = iota((8, LANES), 0) < PACK

    def pack(parts):
        tiles = []
        for g in range(groups):
            at = g * PACK % 8
            first, second = parts[g * PACK // 8]
            if first.shape[0] == PACK:
                tiles.append(jnp.concatenate([first, second], axis=0))
            elif at == 0:
                tiles.append(jnp.where(top, first, pltpu.roll(second, 4, 0)))
            else:
                tiles.append(jnp.where(top, pltpu.roll(first, 4, 0), second))
        return tiles

    def read(load, i):
        parts = []
        for start in range(0, blocks, 8):
            rows = slice(start, min(start + 8, blocks))
            parts.append(
                [load(rows, pl.ds(pl.multiple_of(i * PLANE + h * LANES, LANES), LANES)) for h in range(2)]
            )
        return pack(parts)

    def load_layer(i, carry):
        flow = [read(lambda r, s: flow_ref[c, r, s], i) for c in range(5)]
        for g in range(groups):
            for c, x in enumerate(primitive([f[g] for f in flow])):
                val_ref[g, c, i] = x
        for c in range(5):
            for g, x in enumerate(read(lambda r, s: adj_ref[c, r, s], i)):
                val_ref[g, 5 + c, i] = x
        for g, x in enumerate(read(lambda r, s: flag_ref[r, s], i)):
            solid_ref[g, i] = x.astype(jnp.float32)
        return carry

    lax.fori_loop(0, EDGE, load_layer, 0)


def minmod(a, b):
    return jnp.where(a * b > 0.0, jnp.where(jnp.abs(a) < jnp.abs(b), a, b), 0.0)


def halo_kernel(
    capacity, owner_ref, link_ref, ver_link_ref, flow_hbm, adj_hbm, flag_hbm,
    ret_ref, val_hbm, slope_hbm, solid_hbm, kghost_ref, edge_hbm,
    flow_ref, adj_ref, flag_ref, lat_ref, ver_ref, req_ref, want_ref, index_ref, stage, low_ref, high_ref,
    val, slope, solid_ref, edge,
    ask_sem, asked_sem, send_sem, recv_sem, up_sem, down_sem, own_sem, in_sem, pack_sem,
):
    blocks = flow_ref.shape[1]
    groups = blocks // PACK
    peers = req_ref.shape[0]
    rows = stage.shape[1]
    me = lax.axis_index("blk")
    region = lax.axis_index("grp")
    last = lax.axis_size("grp") - 1
    has_low, has_high = region > 0, region < last

    barrier = pltpu.get_barrier_semaphore()
    for d in range(1, peers):
        pl.semaphore_signal(
            barrier, inc=1, device_id={"blk": lax.rem(me + d, peers)}, device_id_type=MESH
        )
    for there, step in ((has_low, -1), (has_high, 1)):
        @pl.when(there)
        def _():
            pl.semaphore_signal(
                barrier, inc=1, device_id={"grp": region + step}, device_id_type=MESH
            )

    loads = [
        pltpu.make_async_copy(a, b, in_sem.at[at])
        for at, (a, b) in enumerate(((flow_hbm, flow_ref), (adj_hbm, adj_ref), (flag_hbm, flag_ref)))
    ]
    for load in loads:
        load.start()

    holder = iota((peers, LANES), 0)
    column = iota((peers, LANES), 1)

    def ask(b, carry):
        asked, count = carry
        for f in range(4):
            code = link_ref[f, b] // 5 * 4 + (f ^ 1)
            match = holder == owner_ref[f, 0, b]
            asked = jnp.where(match & (column == count), code, asked)
            count = count + match.astype(jnp.int32)
        return asked, count

    nobody = jnp.zeros((peers, LANES), jnp.int32)
    asked, _ = lax.fori_loop(0, blocks, ask, (nobody, nobody))
    for p in range(peers):
        req_ref[p] = asked[p : p + 1]

    def request(d):
        peer = lax.rem(me + d, peers)
        return pltpu.make_async_remote_copy(
            src_ref=req_ref.at[peer],
            dst_ref=want_ref.at[me],
            send_sem=ask_sem.at[d],
            recv_sem=asked_sem.at[d],
            device_id={"blk": peer},
            device_id_type=MESH,
        )

    own = pltpu.make_async_copy(req_ref.at[me], want_ref.at[me], own_sem)
    own.start()
    lane = iota((blocks, LANES), 1)
    slot, spot = lane >> 4, lane & 15

    def layers(ref, c):
        def tile(i, half):
            return ref[c, :, i * PLANE + half * LANES : i * PLANE + (half + 1) * LANES]

        out = {}
        for half in range(2):
            out[0, half] = tile(0, half)
            out[1, half] = tile(EDGE - 1, half)
            low_j = high_j = low_k = high_k = jnp.zeros((blocks, LANES), jnp.float32)
            for i in range(EDGE):
                if i // 8 == half:
                    il = i % 8
                    low_j = jnp.where(slot == il, pltpu.roll(tile(i, 0), il * 16, 1), low_j)
                    high_j = jnp.where(
                        slot == il, pltpu.roll(tile(i, 1), (il * 16 + 16) % LANES, 1), high_j
                    )
                here = tile(i, half)
                low_k = jnp.where(spot == i, pltpu.roll(here, i, 1), low_k)
                high_k = jnp.where(spot == i, pltpu.roll(here, (LANES + i - 15) % LANES, 1), high_k)
            out[2, half], out[3, half], out[4, half], out[5, half] = low_j, high_j, low_k, high_k
        return out

    def put(face, half, c, value):
        where = slice(half * LANES, (half + 1) * LANES)
        if face < 4:
            lat_ref[face, c, :, where] = value
        else:
            ver_ref[face - 4, c, :, where] = value

    loads[0].wait()
    loads[1].wait()
    for c in range(5):
        if c == 2:
            pl.semaphore_wait(
                barrier, peers - 1 + has_low.astype(jnp.int32) + has_high.astype(jnp.int32)
            )
            for d in range(1, peers):
                request(d).start()
        for (face, half), value in layers(flow_ref, c).items():
            put(face, half, c, value)
        for (face, half), value in layers(adj_ref, c).items():
            put(face, half, 5 + c, value)
    for half in range(2):
        where = slice(half * LANES, (half + 1) * LANES)
        for ref, count in ((ver_ref, 2), (lat_ref, 4)):
            for face in range(count):
                prim = primitive([ref[face, c, :, where] for c in range(5)])
                for c in range(1, 5):
                    ref[face, c, :, where] = prim[c]

    def vertical(source, target, sem, step):
        return pltpu.make_async_remote_copy(
            src_ref=ver_ref.at[source],
            dst_ref=target,
            send_sem=sem.at[0],
            recv_sem=sem.at[1],
            device_id={"grp": region + step},
            device_id_type=MESH,
        )

    upward = vertical(1, low_ref, up_sem, 1)
    downward = vertical(0, high_ref, down_sem, -1)

    @pl.when(has_high)
    def _():
        upward.start()

    @pl.when(has_low)
    def _():
        downward.start()

    loads[2].wait()
    pack_cells(flow_ref, adj_ref, flag_ref, val, solid_ref)

    own.wait()
    for d in range(1, peers):
        request(d).wait()
    indices = pltpu.make_async_copy(want_ref, index_ref, own_sem)
    indices.start()
    indices.wait()

    def copy(d):
        peer = lax.rem(me + d, peers)
        return pltpu.make_async_remote_copy(
            src_ref=stage.at[peer],
            dst_ref=ret_ref.at[me],
            send_sem=send_sem.at[d],
            recv_sem=recv_sem.at[d],
            device_id={"blk": peer},
            device_id_type=MESH,
        )

    def gather(peer):
        def one(s, carry):
            code = index_ref[peer, 0, s]
            face, block = code & 3, code >> 2
            for c in range(10):
                x = lat_ref[face, c, pl.ds(block, 1), :]
                for h in range(2):
                    stage[peer, pl.ds(s * 20 + c * 2 + h, 1), :] = x[:, h * LANES : (h + 1) * LANES]
            return carry

        lax.fori_loop(0, capacity, one, 0)

    def send(t, carry):
        sign = 2 * lax.rem(t, 2) - 1
        d = peers // 2 + (t + 1) // 2 * sign
        gather(lax.rem(me + d, peers))
        copy(d).start()
        return carry

    lax.fori_loop(0, peers - 1, send, 0)
    gather(me)
    mine = pltpu.make_async_copy(stage.at[me], ret_ref.at[me], own_sem)
    mine.start()

    packed = [
        pltpu.make_async_copy(val, val_hbm, pack_sem.at[0]),
        pltpu.make_async_copy(solid_ref, solid_hbm, pack_sem.at[1]),
    ]
    for copy_out in packed:
        copy_out.start()

    def far(ref):
        for c in range(10):
            ref[c] = jnp.full(ref.shape[1:], FREESTREAM[c] if c < 5 else 0.0, jnp.float32)

    @pl.when(has_low)
    def _():
        downward.wait_send()
        upward.wait_recv()

    @pl.when(jnp.logical_not(has_low))
    def _():
        far(low_ref)

    @pl.when(has_high)
    def _():
        upward.wait_send()
        downward.wait_recv()

    @pl.when(jnp.logical_not(has_high))
    def _():
        far(high_ref)

    lane = iota((8, LANES), 1)
    row = iota((8, LANES), 0)
    top = row < PACK
    slot, spot = lane >> 4, lane & 15

    def load_ghost(c, carry):
        for b in range(blocks):
            g, at = b // PACK, b % PACK
            for f, ref in enumerate((low_ref, high_ref)):
                x = ref[c, pl.ds(ver_link_ref[f, b] // 5, 1), :]
                kghost_ref[g, f, c, at : at + 1, :] = x[:, :LANES]
                kghost_ref[g, f, c, PACK + at : PACK + at + 1, :] = x[:, LANES:]
        return carry

    lax.fori_loop(0, 10, load_ghost, 0)
    half = row >> 2
    for g in range(groups):
        for f in range(2):
            code = jnp.zeros((8, LANES), jnp.int32)
            for at in range(PACK):
                one = lax.rem(ver_link_ref[f, g * PACK + at], 5)
                one = jnp.where(one == 4, 4, ((one & 1) << 1) + (one >> 1))
                code = jnp.where((row & 3) == at, one, code)
            mine_half = (code == 4) | ((code >> 1) == half)
            quarter = ((4 * half + (slot >> 1)) << 4) + ((code & 1) << 3) + (spot >> 1)
            index = jnp.where(code == 4, lane, quarter)
            for c in range(10):
                x = kghost_ref[g, f, c]
                x = jnp.where(mine_half, x, pltpu.roll(x, 4, 0))
                x = jnp.take_along_axis(x, index, axis=1, mode="promise_in_bounds")
                kghost_ref[g, f, c] = x

    def slopes_of(g, carry):
        def slopes(i, inner):
            below, above = jnp.maximum(i - 1, 0), jnp.minimum(i + 1, EDGE - 1)
            turn = (i & 7) * 16
            held = slot == jnp.where(top, i & 7, (i + 7) & 7)
            for c in range(10):
                own = val[g, c, i]
                y = pltpu.roll(own, LANES - 16, 1)
                next_j = jnp.where(slot == 7, pltpu.roll(y, 4, 0), y)
                y = pltpu.roll(own, 16, 1)
                prev_j = jnp.where(slot == 0, pltpu.roll(y, 4, 0), y)
                next_k = jnp.where(
                    spot == 15,
                    pltpu.roll(kghost_ref[g, 1, c], 15 - i, 1),
                    pltpu.roll(own, LANES - 1, 1),
                )
                prev_k = jnp.where(
                    spot == 0,
                    pltpu.roll(kghost_ref[g, 0, c], lax.rem(LANES - i, LANES), 1),
                    pltpu.roll(own, 1, 1),
                )
                up, down = next_j - own, own - prev_j
                slope[g, 0, c, i] = 0.25 * minmod(val[g, c, above] - own, own - val[g, c, below])
                slope[g, 1, c, i] = 0.25 * minmod(up, down)
                slope[g, 2, c, i] = 0.25 * minmod(next_k - own, own - prev_k)
                inside = pltpu.roll(jnp.where(top, up, down), turn, 1)
                edge[g, 0, c, i >> 3] = jnp.where(held, inside, edge[g, 0, c, i >> 3])
                edge[g, 1, c, i >> 3] = jnp.where(held, pltpu.roll(own, turn, 1), edge[g, 1, c, i >> 3])
            return inner

        for at in range(2):
            for c in range(10):
                for p in range(2):
                    edge[g, at, c, p] = jnp.zeros((8, LANES), jnp.float32)
        lax.fori_loop(0, EDGE, slopes, 0)
        out(g).start()
        return carry

    def out(g):
        return pltpu.make_async_copy(slope.at[g], slope_hbm.at[g], pack_sem.at[3 + g])

    lax.fori_loop(0, groups, slopes_of, 0)
    edges = pltpu.make_async_copy(edge, edge_hbm, pack_sem.at[2])
    edges.start()

    def finish(d, carry):
        copy(d).wait()
        return carry

    lax.fori_loop(1, peers, finish, 0)
    mine.wait()
    for copy_out in packed:
        copy_out.wait()
    edges.wait()
    for g in range(groups):
        out(g).wait()


def basic(state):
    rho, u, v, w, p = state
    inv_root = lax.rsqrt(rho)
    root = rho * inv_root
    enth = (3.5 * p) * (inv_root * inv_root) + 0.5 * (u * u + v * v + w * w)
    return [root, u, v, w, p, enth]


def full(parts):
    root, u, v, w, p, enth = parts
    return (root, (u, v, w), p, enth, (root * u, root * v, root * w), root * enth)


def roe(left, right, n):
    root_l, vel_l, p_l, h_l, rv_l, rh_l = left
    root_r, vel_r, p_r, h_r, rv_r, rh_r = right
    r = lax.rsqrt(root_l + root_r)
    inv = r * r
    vel = [(a + b) * inv for a, b in zip(rv_l, rv_r)]
    enth = (rh_l + rh_r) * inv
    un = vel[n]
    c_sq = 0.4 * enth - 0.2 * (vel[0] * vel[0] + vel[1] * vel[1] + vel[2] * vel[2])
    inv_c = lax.rsqrt(c_sq)
    c = c_sq * inv_c
    speed = jnp.abs(un)
    mach = speed * inv_c
    t = 1.0 - mach
    z = jnp.maximum(0.2 - jnp.abs(t), 0.0)
    w = (1.25 * z) * z
    even = jnp.maximum(t, 0.0) + w
    odd = jnp.minimum(mach, 1.0) - w
    odd = jnp.where(un < 0.0, -odd, odd)
    dp = p_r - p_l
    a = dp * inv_c
    b = (root_l * root_r) * (vel_r[n] - vel_l[n])
    first = (even * a + odd * b) * inv
    second = c * (odd * a + even * b)
    m_l = root_l * (root_l * (vel_l[n] + speed) - first)
    m_r = root_r * (root_r * (vel_r[n] - speed) - first)
    out = [m_l + m_r] + [m_l * x + m_r * y for x, y in zip(vel_l, vel_r)]
    out[1 + n] = out[1 + n] + ((p_l + p_r) - second)
    out.append((m_l * h_l + m_r * h_r) + (speed * dp - second * un))
    return out


def quads(base, q1, q2):
    low = [b - q for b, q in zip(base, q1)]
    high = [b + q for b, q in zip(base, q1)]
    return [
        basic([b - q for b, q in zip(low, q2)]),
        basic([b + q for b, q in zip(low, q2)]),
        basic([b - q for b, q in zip(high, q2)]),
        basic([b + q for b, q in zip(high, q2)]),
    ]


def moments(lefts, rights, n):
    f = [roe(a, b, n) for a, b in zip(lefts, rights)]
    zero, first, second = [], [], []
    for c in range(5):
        low, high = f[0][c] + f[1][c], f[2][c] + f[3][c]
        zero.append(low + high)
        first.append(high - low)
        second.append((f[1][c] - f[0][c]) + (f[3][c] - f[2][c]))
    return zero + first + second


def dot(a, b):
    total = a[0] * b[0]
    for x, y in zip(a[1:], b[1:]):
        total = total + x * y
    return total


def main_kernel(
    owner_ref, link_ref,
    ret_hbm, kghost_hbm, val_hbm, slope_hbm, solid_hbm, edge_hbm,
    out_ref,
    ret_ref, kghost, val, slope, solid, edge, sems, place_ref, count_ref,
    raw_i, raw_j, fixed, jedge, kedge, carry_hi, carry_sum, first_k, first_j, start_k, start_j, total_ref, found_ref,
):
    blocks = link_ref.shape[1]
    groups = blocks // PACK
    peers = count_ref.shape[0]
    rows = ret_ref.shape[0] // peers
    lane = iota((8, LANES), 1)
    row = iota((8, LANES), 0)
    top = row < PACK
    slot, spot = lane >> 4, lane & 15
    nothing = jnp.zeros((8, LANES), jnp.float32)

    returned = pltpu.make_async_copy(ret_hbm, ret_ref, sems.at[0])
    returned.start()
    shared = [
        pltpu.make_async_copy(kghost_hbm, kghost, sems.at[1]),
        pltpu.make_async_copy(solid_hbm, solid.at[:, pl.ds(1, EDGE)], sems.at[2]),
        pltpu.make_async_copy(edge_hbm, edge, sems.at[3]),
    ]
    for copy in shared:
        copy.start()

    def cells(g):
        return (
            pltpu.make_async_copy(val_hbm.at[g], val.at[g], sems.at[4 + 2 * g]),
            pltpu.make_async_copy(slope_hbm.at[g], slope.at[g], sems.at[5 + 2 * g]),
        )

    for g in range(groups):
        for copy in cells(g):
            copy.start()

    def clear(p, carry):
        count_ref[p] = 0
        return carry

    lax.fori_loop(0, peers, clear, 0)

    def plan(b, carry):
        for f in range(4):
            owner = owner_ref[f, 0, b]
            at = count_ref[owner]
            count_ref[owner] = at + 1
            place_ref[b * 4 + f] = owner * rows + at * 20
        return carry

    lax.fori_loop(0, blocks, plan, 0)
    returned.wait()

    def load_ghost(b, carry):
        g, at = b // PACK, lax.rem(b, PACK)
        for f in range(4):
            code = lax.rem(link_ref[f, b], 5)
            base = place_ref[b * 4 + f]
            for h in range(2):
                from_row = base + jnp.where(code == 4, h, code >> 1)
                for c in range(10):
                    x = ret_ref[pl.ds(from_row + 2 * c, 1), :]
                    if f < 2:
                        raw_i[g, f, c, pl.ds(h * PACK + at, 1), :] = x
                    else:
                        raw_j[g, c, h, pl.ds((f - 2) * PACK + at, 1), :] = x
        return carry

    lax.fori_loop(0, blocks, load_ghost, 0)

    def codes(g, face_of_half):
        code = jnp.zeros((8, LANES), jnp.int32)
        for r in range(8):
            one = lax.rem(link_ref[face_of_half[r // PACK], g * PACK + r % PACK], 5)
            code = jnp.where(row == r, one, code)
        return code

    def picks(code, half, at):
        quarter = ((4 * half + (at >> 1)) << 4) + ((code & 1) << 3) + (spot >> 1)
        return jnp.where(code == 4, at * 16 + spot, quarter)

    def pick(x, index):
        return jnp.take_along_axis(x, index, axis=1, mode="promise_in_bounds")

    for g in range(groups):
        for f in range(2):
            index = picks(codes(g, (f, f)), row >> 2, slot)
            for c in range(10):
                raw_i[g, f, c] = pick(raw_i[g, f, c], index)
        code = codes(g, (2, 3))
        for p in range(2):
            index = picks(code, p, jnp.where(top, slot, (slot + 1) & 7))
            for c in range(10):
                raw_j[g, c, p] = pick(raw_j[g, c, p], index)
        solid[g, 0] = nothing
        solid[g, EDGE + 1] = nothing
    for copy in shared:
        copy.wait()

    def next_k(x):
        return pltpu.roll(x, LANES - 1, 1)

    def prev_k(x):
        return pltpu.roll(x, 1, 1)

    def next_j(x, edge_x):
        y = pltpu.roll(x, LANES - 16, 1)
        z = pltpu.roll(y, 4, 0)
        if edge_x is not None:
            z = jnp.where(top, z, edge_x)
        return jnp.where(slot == 7, z, y)

    def prev_j(x):
        y = pltpu.roll(x, 16, 1)
        return jnp.where(slot == 0, pltpu.roll(y, 4, 0), y)

    last_j = (slot == 7) & jnp.logical_not(top)
    zero_j = (slot == 0) & top
    rim_j = last_j | zero_j

    def group(g, carry):
        for copy in cells(g):
            copy.wait()
        for c in range(10):
            for p in range(2):
                own, ghost = edge[g, 1, c, p], raw_j[g, c, p]
                other = jnp.where(top, own - ghost, ghost - own)
                fixed[c, p] = 0.25 * minmod(edge[g, 0, c, p], other)
            first, second = val[g, c, 0], val[g, c, 1]
            slope[g, 0, c, 0] = 0.25 * minmod(second - first, first - raw_i[g, 0, c])
            first, second = val[g, c, EDGE - 2], val[g, c, EDGE - 1]
            slope[g, 0, c, EDGE - 1] = 0.25 * minmod(raw_i[g, 1, c] - second, second - first)
        for p in range(2):
            for at, x in enumerate(basic([raw_j[g, c, p] for c in range(5)])):
                jedge[at, p] = x
        for at, x in enumerate(basic([kghost[g, 1, c] for c in range(5)])):
            kedge[at] = x
        for at, x in enumerate(basic([raw_i[g, 0, c] for c in range(5)])):
            for s in range(4):
                carry_hi[s, at] = x
        carry_sum[0] = nothing
        carry_sum[1] = nothing

        def join(at, lefts, rights):
            f = moments(lefts, rights, 0)
            below = jnp.maximum(at - 1, 0)
            outer = [val[g, 5 + c, below] + slope[g, 0, 5 + c, below] for c in range(5)]
            aq1 = [slope[g, 1, 5 + c, below] for c in range(5)]
            aq2 = [slope[g, 2, 5 + c, below] for c in range(5)]
            return f, outer, aq1, aq2

        def layer(i, inner):
            turn = lax.rem(LANES - (i & 7) * 16, LANES)
            v = [val[g, c, i] for c in range(5)]
            av = [val[g, 5 + c, i] for c in range(5)]
            q = [[slope[g, d, c, i] for c in range(5)] for d in range(3)]
            aq = [[slope[g, d, 5 + c, i] for c in range(5)] for d in range(3)]
            for c in range(5):
                q[1][c] = jnp.where(rim_j, pltpu.roll(fixed[c, i >> 3], turn, 1), q[1][c])
                aq[1][c] = jnp.where(rim_j, pltpu.roll(fixed[5 + c, i >> 3], turn, 1), aq[1][c])
                slope[g, 1, 5 + c, i] = aq[1][c]
            child, part = {}, {}
            for a in range(2):
                base = [x + y if a else x - y for x, y in zip(v, q[0])]
                for at, state in enumerate(quads(base, q[1], q[2])):
                    part[a, at >> 1, at & 1] = state
                    child[a, at >> 1, at & 1] = full(state)

            def side(store, n, high):
                order = [(s, t) for s in range(2) for t in range(2)]
                return [store[tuple([*st[:n], high, *st[n:]])] for st in order]

            own_solid = solid[g, 1 + i]
            total = nothing
            wall_above = nothing
            for n in range(3):
                t1, t2 = [a for a in range(3) if a != n]
                f = [roe(a, b, n) for a, b in zip(side(child, n, 0), side(child, n, 1))]
                inside = [(f[0][c] + f[1][c]) + (f[2][c] + f[3][c]) for c in range(5)]
                total = total - 2.0 * dot(aq[n], inside)
                outer = [x + y for x, y in zip(av, aq[n])]
                inner_side = [x - y for x, y in zip(av, aq[n])]
                cross = aq[t1][1 + n] * q[t1][4] + aq[t2][1 + n] * q[t2][4]
                wall_up = 8.0 * (outer[1 + n] * (v[4] + q[n][4]) + cross)
                wall_down = 8.0 * (inner_side[1 + n] * (v[4] - q[n][4]) + cross)
                if n == 0:
                    lefts = [full([carry_hi[s, at] for at in range(6)]) for s in range(4)]
                    below, before, b1, b2 = join(i, lefts, side(child, 0, 0))
                    for s, state in enumerate(side(part, 0, 1)):
                        for at in range(6):
                            carry_hi[s, at] = state[at]
                    ahead = dot([*before, *b1, *b2], below)
                    total_ref[i] = carry_sum[0] + jnp.where(own_solid > 0.5, carry_sum[1], ahead)
                    lower = dot([*inner_side, *aq[1], *aq[2]], below)
                    total = total - jnp.where(solid[g, i] > 0.5, wall_down, lower)
                    wall_above = wall_up
                    continue
                if n == 1:
                    rims = [pltpu.roll(jedge[at, i >> 3], turn, 1) for at in range(6)]
                    rights = [
                        full([next_j(x, rim) for x, rim in zip(state, rims)]) for state in side(part, 1, 0)
                    ]
                    above = moments(side(child, 1, 1), rights, 1)
                    below = [prev_j(x) for x in above]
                    up_solid = jnp.where(last_j, 0.0, next_j(own_solid, None))
                    down_solid = prev_j(own_solid)
                    rim = zero_j
                else:
                    rims = [pltpu.roll(kedge[at], 15 - i, 1) for at in range(6)]
                    rights = [
                        full([jnp.where(spot == 15, rim, next_k(x)) for x, rim in zip(state, rims)])
                        for state in side(part, 2, 0)
                    ]
                    above = moments(side(child, 2, 1), rights, 2)
                    below = [prev_k(x) for x in above]
                    up_solid = jnp.where(spot == 15, 0.0, next_k(own_solid))
                    down_solid = prev_k(own_solid)
                    rim = spot == 0
                upper = dot([*outer, *aq[t1], *aq[t2]], above)
                lower = dot([*inner_side, *aq[t1], *aq[t2]], below)
                lower = jnp.where(rim, 0.0, jnp.where(down_solid > 0.5, wall_down, lower))
                total = total + (jnp.where(up_solid > 0.5, wall_up, upper) - lower)
                base = [x - y for x, y in zip(v, q[n])]
                if n == 1:
                    held = (slot == (i & 7)) & top
                    shift = (i & 7) * 16
                else:
                    held = spot == i
                    shift = i
                for at, x in enumerate([*base, *q[t1], *q[t2], *inner_side, *aq[t1], *aq[t2]]):
                    x = pltpu.roll(x, shift, 1)
                    ref = first_j.at[at, i >> 3] if n == 1 else first_k.at[at]
                    pltpu.store(ref, x, mask=held)
            carry_sum[0] = total
            carry_sum[1] = wall_above
            return inner

        lax.fori_loop(0, EDGE, layer, 0)

        lefts = [full([carry_hi[s, at] for at in range(6)]) for s in range(4)]
        ghost = full(basic([raw_i[g, 1, c] for c in range(5)]))
        below, before, b1, b2 = join(EDGE, lefts, [ghost] * 4)
        total_ref[EDGE] = carry_sum[0] + dot([*before, *b1, *b2], below)

        def start(n, left, x):
            f = moments([full(basic(left))] * 4, [full(s) for s in quads(x[0:5], x[5:10], x[10:15])], n)
            return dot(x[15:30], f)

        start_k[...] = start(2, [kghost[g, 0, c] for c in range(5)], [first_k[at] for at in range(30)])
        found = start(
            1,
            [jnp.where(top, raw_j[g, c, 0], pltpu.roll(raw_j[g, c, 1], 4, 0)) for c in range(5)],
            [jnp.where(top, first_j[at, 0], pltpu.roll(first_j[at, 1], 4, 0)) for at in range(30)],
        )
        start_j[0] = found
        start_j[1] = pltpu.roll(found, 4, 0)

        def store(i, inner):
            turn = lax.rem(LANES - (i & 7) * 16, LANES)
            low_k = pltpu.roll(start_k[...], lax.rem(LANES - i, LANES), 1)
            low_j = pltpu.roll(start_j[i >> 3], turn, 1)
            x = total_ref[1 + i]
            x = x - jnp.where(spot == 0, low_k, 0.0) - jnp.where(zero_j, low_j, 0.0)
            found_ref[g, i] = jnp.where(solid[g, 1 + i] > 0.5, 0.0, 0.5 * jnp.abs(x))
            return inner

        lax.fori_loop(0, EDGE, store, 0)
        return carry

    lax.fori_loop(0, groups, group, 0)

    def write(i, carry):
        for g in range(groups):
            x = found_ref[g, i]
            for h in range(2):
                out_ref[
                    g * PACK : (g + 1) * PACK,
                    pl.ds(pl.multiple_of(i * PLANE + h * LANES, LANES), LANES),
                ] = x[h * PACK : (h + 1) * PACK]
        return carry

    lax.fori_loop(0, EDGE, write, 0)


def local(flow, adjoint, cut_flag, lateral_owner, lateral_link, vertical_link):
    blocks = flow.shape[0]
    groups = blocks // PACK
    peers = lax.axis_size("blk")
    capacity = max(2, 6 * blocks // peers)
    flow_t = jnp.transpose(flow, (1, 0, 2))
    adj_t = jnp.transpose(adjoint, (1, 0, 2))
    f32 = functools.partial(jax.ShapeDtypeStruct, dtype=jnp.float32)
    tile = functools.partial(pltpu.VMEM, dtype=jnp.float32)

    owner_t = jnp.transpose(lateral_owner, (1, 2, 0))
    link_t, ver_link_t = lateral_link.T, vertical_link.T
    rows = -(-capacity * 20 // 8) * 8
    received = (peers, rows, LANES)
    cells = (groups, 10, EDGE, 8, LANES)
    slopes = (groups, 3, 10, EDGE, 8, LANES)
    flags = (groups, EDGE, 8, LANES)
    kghosts = (groups, 2, 10, 8, LANES)
    edges = (groups, 2, 10, 2, 8, LANES)
    returned, packed, slope, solid, kghost, edge = pl.pallas_call(
        functools.partial(halo_kernel, capacity),
        out_shape=tuple(f32(s) for s in (received, cells, slopes, flags, kghosts, edges)),
        in_specs=[SMEM] * 3 + [HBM] * 3,
        out_specs=(HBM, HBM, HBM, HBM, VMEM, HBM),
        scratch_shapes=[
            tile((5, blocks, EDGE * PLANE)),
            tile((5, blocks, EDGE * PLANE)),
            pltpu.VMEM((blocks, EDGE * PLANE), jnp.int32),
            tile((4, 10, blocks, PLANE)),
            tile((2, 10, blocks, PLANE)),
            pltpu.VMEM((peers, 1, LANES), jnp.int32),
            pltpu.VMEM((peers, 1, LANES), jnp.int32),
            pltpu.SMEM((peers, 1, LANES), jnp.int32),
            tile(received),
            tile((10, blocks, PLANE)),
            tile((10, blocks, PLANE)),
            tile(cells),
            tile(slopes),
            tile(flags),
            tile(edges),
            *[pltpu.SemaphoreType.DMA((peers,))] * 4,
            pltpu.SemaphoreType.DMA((2,)),
            pltpu.SemaphoreType.DMA((2,)),
            pltpu.SemaphoreType.DMA,
            pltpu.SemaphoreType.DMA((3,)),
            pltpu.SemaphoreType.DMA((3 + groups,)),
        ],
        compiler_params=pltpu.CompilerParams(
            collective_id=0, has_side_effects=True, vmem_limit_bytes=63 * 1024 * 1024
        ),
        name="halo",
    )(owner_t, link_t, ver_link_t, flow_t, adj_t, cut_flag)

    return pl.pallas_call(
        main_kernel,
        out_shape=f32((blocks, EDGE * PLANE)),
        in_specs=[SMEM] * 2 + [HBM] * 6,
        out_specs=VMEM,
        scratch_shapes=[
            tile((peers * rows, LANES)),
            tile(kghosts),
            tile(cells),
            tile(slopes),
            tile((groups, EDGE + 2, 8, LANES)),
            tile(edges),
            pltpu.SemaphoreType.DMA((4 + 2 * groups,)),
            pltpu.SMEM((blocks * 4,), jnp.int32),
            pltpu.SMEM((peers,), jnp.int32),
            tile((groups, 2, 10, 8, LANES)),
            tile((groups, 10, 2, 8, LANES)),
            tile((10, 2, 8, LANES)),
            tile((6, 2, 8, LANES)),
            tile((6, 8, LANES)),
            tile((4, 6, 8, LANES)),
            tile((2, 8, LANES)),
            tile((30, 8, LANES)),
            tile((30, 2, 8, LANES)),
            tile((8, LANES)),
            tile((2, 8, LANES)),
            tile((EDGE + 1, 8, LANES)),
            tile(flags),
        ],
        compiler_params=pltpu.CompilerParams(vmem_limit_bytes=63 * 1024 * 1024),
        name="indicator",
    )(
        owner_t, link_t,
        returned.reshape(peers * rows, LANES), kghost, packed, slope, solid, edge,
    )


def solution(mesh):
    spec3 = P(("blk", "grp"), None, None)
    spec2 = P(("blk", "grp"), None)
    return jax.shard_map(
        local,
        mesh=mesh,
        in_specs=(spec3, spec3, spec2, spec3, spec2, spec2),
        out_specs=spec2,
        check_vma=False,
    )
```

```python
import functools

import jax
import jax.numpy as jnp
from jax import lax
from jax.experimental import pallas as pl
from jax.experimental.pallas import tpu as pltpu
from jax.sharding import PartitionSpec as P

EDGE = 16
PLANE = EDGE * EDGE
LANES = 128
PACK = 4
FREESTREAM = (1.0, 0.0, 0.0, 0.3, 1.0)
VMEM = pl.BlockSpec(memory_space=pltpu.VMEM)
SMEM = pl.BlockSpec(memory_space=pltpu.SMEM)
HBM = pl.BlockSpec(memory_space=pltpu.HBM)
MESH = pl.DeviceIdType.MESH


def iota(shape, dim):
    return lax.broadcasted_iota(jnp.int32, shape, dim)


def primitive(state):
    density, mom, energy = state[0], state[1:4], state[4]
    root = lax.rsqrt(density)
    inverse = root * root
    vel = [m * inverse for m in mom]
    square = vel[0] * vel[0] + vel[1] * vel[1] + vel[2] * vel[2]
    return [density, *vel, 0.4 * (energy - 0.5 * density * square)]


def pack_cells(flow_ref, adj_ref, flag_ref, val_ref, solid_ref):
    blocks = flow_ref.shape[1]
    groups = blocks // PACK
    top = iota((8, LANES), 0) < PACK

    def pack(parts):
        tiles = []
        for g in range(groups):
            at = g * PACK % 8
            first, second = parts[g * PACK // 8]
            if first.shape[0] == PACK:
                tiles.append(jnp.concatenate([first, second], axis=0))
            elif at == 0:
                tiles.append(jnp.where(top, first, pltpu.roll(second, 4, 0)))
            else:
                tiles.append(jnp.where(top, pltpu.roll(first, 4, 0), second))
        return tiles

    def read(load, i):
        parts = []
        for start in range(0, blocks, 8):
            rows = slice(start, min(start + 8, blocks))
            parts.append(
                [load(rows, pl.ds(pl.multiple_of(i * PLANE + h * LANES, LANES), LANES)) for h in range(2)]
            )
        return pack(parts)

    def load_layer(i, carry):
        flow = [read(lambda r, s: flow_ref[c, r, s], i) for c in range(5)]
        for g in range(groups):
            for c, x in enumerate(primitive([f[g] for f in flow])):
                val_ref[g, c, i] = x
        for c in range(5):
            for g, x in enumerate(read(lambda r, s: adj_ref[c, r, s], i)):
                val_ref[g, 5 + c, i] = x
        for g, x in enumerate(read(lambda r, s: flag_ref[r, s], i)):
            solid_ref[g, i] = x.astype(jnp.float32)
        return carry

    lax.fori_loop(0, EDGE, load_layer, 0)


def minmod(a, b):
    return jnp.where(a * b > 0.0, jnp.where(jnp.abs(a) < jnp.abs(b), a, b), 0.0)


def basic(state):
    rho, u, v, w, p = state
    inv_root = lax.rsqrt(rho)
    root = rho * inv_root
    enth = (3.5 * p) * (inv_root * inv_root) + 0.5 * (u * u + v * v + w * w)
    return [root, u, v, w, p, enth]


def full(parts):
    root, u, v, w, p, enth = parts
    return (root, (u, v, w), p, enth, (root * u, root * v, root * w), root * enth)


def roe(left, right, n):
    root_l, vel_l, p_l, h_l, rv_l, rh_l = left
    root_r, vel_r, p_r, h_r, rv_r, rh_r = right
    r = lax.rsqrt(root_l + root_r)
    inv = r * r
    vel = [(a + b) * inv for a, b in zip(rv_l, rv_r)]
    enth = (rh_l + rh_r) * inv
    un = vel[n]
    c_sq = 0.4 * enth - 0.2 * (vel[0] * vel[0] + vel[1] * vel[1] + vel[2] * vel[2])
    inv_c = lax.rsqrt(c_sq)
    c = c_sq * inv_c
    speed = jnp.abs(un)
    mach = speed * inv_c
    t = 1.0 - mach
    z = jnp.maximum(0.2 - jnp.abs(t), 0.0)
    w = (1.25 * z) * z
    even = jnp.maximum(t, 0.0) + w
    odd = jnp.minimum(mach, 1.0) - w
    odd = jnp.where(un < 0.0, -odd, odd)
    dp = p_r - p_l
    a = dp * inv_c
    b = (root_l * root_r) * (vel_r[n] - vel_l[n])
    first = (even * a + odd * b) * inv
    second = c * (odd * a + even * b)
    m_l = root_l * (root_l * (vel_l[n] + speed) - first)
    m_r = root_r * (root_r * (vel_r[n] - speed) - first)
    out = [m_l + m_r] + [m_l * x + m_r * y for x, y in zip(vel_l, vel_r)]
    out[1 + n] = out[1 + n] + ((p_l + p_r) - second)
    out.append((m_l * h_l + m_r * h_r) + (speed * dp - second * un))
    return out


def quads(base, q1, q2):
    low = [b - q for b, q in zip(base, q1)]
    high = [b + q for b, q in zip(base, q1)]
    return [
        basic([b - q for b, q in zip(low, q2)]),
        basic([b + q for b, q in zip(low, q2)]),
        basic([b - q for b, q in zip(high, q2)]),
        basic([b + q for b, q in zip(high, q2)]),
    ]


def moments(lefts, rights, n):
    f = [roe(a, b, n) for a, b in zip(lefts, rights)]
    zero, first, second = [], [], []
    for c in range(5):
        low, high = f[0][c] + f[1][c], f[2][c] + f[3][c]
        zero.append(low + high)
        first.append(high - low)
        second.append((f[1][c] - f[0][c]) + (f[3][c] - f[2][c]))
    return zero + first + second


def dot(a, b):
    total = a[0] * b[0]
    for x, y in zip(a[1:], b[1:]):
        total = total + x * y
    return total


def whole_kernel(
    capacity, owner_ref, link_ref, ver_link_ref, flow_hbm, adj_hbm, flag_hbm, out_ref,
    flow_ref, adj_ref, flag_ref, lat_ref, ver_ref, req_ref, want_ref, index_ref, spot_ref, place_ref,
    stage, ret_ref, low_ref, high_ref,
    val, slope, solid_ref, kghost, cval, cslope,
    raw_i, raw_j, jedge, kedge, carry_hi, carry_sum, first_k, total_ref, found_ref,
    ask_sem, asked_sem, send_sem, recv_sem, up_sem, down_sem, own_sem, in_sem,
):
    blocks = flow_ref.shape[1]
    groups = blocks // PACK
    peers = req_ref.shape[0]
    rows = stage.shape[1]
    used = capacity * 20
    me = lax.axis_index("blk")
    region = lax.axis_index("grp")
    last = lax.axis_size("grp") - 1
    has_low, has_high = region > 0, region < last

    barrier = pltpu.get_barrier_semaphore()
    for d in range(1, peers):
        pl.semaphore_signal(
            barrier, inc=1, device_id={"blk": lax.rem(me + d, peers)}, device_id_type=MESH
        )
    for there, step in ((has_low, -1), (has_high, 1)):
        @pl.when(there)
        def _():
            pl.semaphore_signal(
                barrier, inc=1, device_id={"grp": region + step}, device_id_type=MESH
            )

    loads = [
        pltpu.make_async_copy(a, b, in_sem.at[at])
        for at, (a, b) in enumerate(((flow_hbm, flow_ref), (adj_hbm, adj_ref), (flag_hbm, flag_ref)))
    ]
    for load in loads:
        load.start()

    holder = iota((peers, LANES), 0)
    column = iota((peers, LANES), 1)

    def ask(b, carry):
        asked, count, placed = carry
        for f in range(4):
            code = link_ref[f, b] // 5 * 4 + (f ^ 1)
            match = holder == owner_ref[f, 0, b]
            asked = jnp.where(match & (column == count), code, asked)
            placed = jnp.where(match & (column == b * 4 + f), holder * rows + count * 20, placed)
            count = count + match.astype(jnp.int32)
        return asked, count, placed

    nobody = jnp.zeros((peers, LANES), jnp.int32)
    asked, _, placed = lax.fori_loop(0, blocks, ask, (nobody, nobody, nobody))
    for p in range(peers):
        req_ref[p] = asked[p : p + 1]
    spot_ref[...] = jnp.sum(placed, axis=0, keepdims=True)
    places = pltpu.make_async_copy(spot_ref, place_ref, in_sem.at[3])
    places.start()

    def request(d):
        peer = lax.rem(me + d, peers)
        return pltpu.make_async_remote_copy(
            src_ref=req_ref.at[peer],
            dst_ref=want_ref.at[me],
            send_sem=ask_sem.at[d],
            recv_sem=asked_sem.at[d],
            device_id={"blk": peer},
            device_id_type=MESH,
        )

    own = pltpu.make_async_copy(req_ref.at[me], want_ref.at[me], own_sem)
    own.start()
    lane = iota((blocks, LANES), 1)
    slot, spot = lane >> 4, lane & 15

    def layers(ref, c):
        def tile(i, half):
            return ref[c, :, i * PLANE + half * LANES : i * PLANE + (half + 1) * LANES]

        out = {}
        for half in range(2):
            out[0, half] = tile(0, half)
            out[1, half] = tile(EDGE - 1, half)
            low_j = high_j = low_k = high_k = jnp.zeros((blocks, LANES), jnp.float32)
            for i in range(EDGE):
                if i // 8 == half:
                    il = i % 8
                    low_j = jnp.where(slot == il, pltpu.roll(tile(i, 0), il * 16, 1), low_j)
                    high_j = jnp.where(
                        slot == il, pltpu.roll(tile(i, 1), (il * 16 + 16) % LANES, 1), high_j
                    )
                here = tile(i, half)
                low_k = jnp.where(spot == i, pltpu.roll(here, i, 1), low_k)
                high_k = jnp.where(spot == i, pltpu.roll(here, (LANES + i - 15) % LANES, 1), high_k)
            out[2, half], out[3, half], out[4, half], out[5, half] = low_j, high_j, low_k, high_k
        return out

    def put(face, half, c, value):
        where = slice(half * LANES, (half + 1) * LANES)
        if face < 4:
            lat_ref[face, c, :, where] = value
        else:
            ver_ref[face - 4, c, :, where] = value

    loads[0].wait()
    loads[1].wait()
    def split(c, carry):
        @pl.when(c == 2)
        def _():
            pl.semaphore_wait(
                barrier, peers - 1 + has_low.astype(jnp.int32) + has_high.astype(jnp.int32)
            )
            for d in range(1, peers):
                request(d).start()

        for (face, half), value in layers(flow_ref, c).items():
            put(face, half, c, value)
        for (face, half), value in layers(adj_ref, c).items():
            put(face, half, 5 + c, value)
        return carry

    lax.fori_loop(0, 5, split, 0)
    for half in range(2):
        where = slice(half * LANES, (half + 1) * LANES)
        for ref, count in ((ver_ref, 2), (lat_ref, 4)):
            for face in range(count):
                prim = primitive([ref[face, c, :, where] for c in range(5)])
                for c in range(1, 5):
                    ref[face, c, :, where] = prim[c]

    def vertical(source, target, sem, step):
        return pltpu.make_async_remote_copy(
            src_ref=ver_ref.at[source],
            dst_ref=target,
            send_sem=sem.at[0],
            recv_sem=sem.at[1],
            device_id={"grp": region + step},
            device_id_type=MESH,
        )

    upward = vertical(1, low_ref, up_sem, 1)
    downward = vertical(0, high_ref, down_sem, -1)

    @pl.when(has_high)
    def _():
        upward.start()

    @pl.when(has_low)
    def _():
        downward.start()

    loads[2].wait()
    pack_cells(flow_ref, adj_ref, flag_ref, val, solid_ref)

    own.wait()
    for d in range(1, peers):
        request(d).wait()
    indices = pltpu.make_async_copy(want_ref, index_ref, own_sem)
    indices.start()
    indices.wait()

    def copy(d):
        peer = lax.rem(me + d, peers)
        return pltpu.make_async_remote_copy(
            src_ref=stage.at[peer, pl.ds(0, used)],
            dst_ref=ret_ref.at[pl.ds(pl.multiple_of(me * rows, 8), used)],
            send_sem=send_sem.at[d],
            recv_sem=recv_sem.at[d],
            device_id={"blk": peer},
            device_id_type=MESH,
        )

    def gather(peer):
        def one(s, carry):
            code = index_ref[peer, 0, s]
            face, block = code & 3, code >> 2
            for c in range(10):
                x = lat_ref[face, c, pl.ds(block, 1), :]
                for h in range(2):
                    stage[peer, pl.ds(s * 20 + c * 2 + h, 1), :] = x[:, h * LANES : (h + 1) * LANES]
            return carry

        lax.fori_loop(0, capacity, one, 0)

    def send(t, carry):
        sign = 2 * lax.rem(t, 2) - 1
        d = peers // 2 + (t + 1) // 2 * sign
        gather(lax.rem(me + d, peers))
        copy(d).start()
        return carry

    lax.fori_loop(0, peers - 1, send, 0)
    gather(me)
    mine = pltpu.make_async_copy(
        stage.at[me, pl.ds(0, used)], ret_ref.at[pl.ds(pl.multiple_of(me * rows, 8), used)], own_sem
    )
    mine.start()

    def far(ref):
        for c in range(10):
            ref[c] = jnp.full(ref.shape[1:], FREESTREAM[c] if c < 5 else 0.0, jnp.float32)

    @pl.when(has_low)
    def _():
        downward.wait_send()
        upward.wait_recv()

    @pl.when(jnp.logical_not(has_low))
    def _():
        far(low_ref)

    @pl.when(has_high)
    def _():
        upward.wait_send()
        downward.wait_recv()

    @pl.when(jnp.logical_not(has_high))
    def _():
        far(high_ref)

    lane = iota((8, LANES), 1)
    row = iota((8, LANES), 0)
    top = row < PACK
    slot, spot = lane >> 4, lane & 15


    def load_vertical(b, carry):
        g, at = b // PACK, lax.rem(b, PACK)
        for f, ref in enumerate((low_ref, high_ref)):
            link = ver_link_ref[f, b]
            code, block = lax.rem(link, 5), link // 5
            halves = [jnp.where(code == 4, h, code & 1) == 1 for h in range(2)]
            for c in range(10):
                x = ref[c, pl.ds(block, 1), :]
                for h, upper in enumerate(halves):
                    y = jnp.where(upper, x[:, LANES:], x[:, :LANES])
                    kghost[g, f, c, pl.ds(h * PACK + at, 1), :] = y
        return carry

    lax.fori_loop(0, blocks, load_vertical, 0)

    def codes(one_of, g, faces):
        code = jnp.zeros((8, LANES), jnp.int32)
        for r in range(8):
            code = jnp.where(row == r, one_of(faces[r // PACK], g * PACK + r % PACK), code)
        return code

    def picks(code, half, at):
        quarter = ((4 * half + (at >> 1)) << 4) + ((code & 1) << 3) + (spot >> 1)
        return jnp.where(code == 4, at * 16 + spot, quarter)

    def pick(x, index):
        return jnp.take_along_axis(x, index, axis=1, mode="promise_in_bounds")

    def vertical_code(f, b):
        one = lax.rem(ver_link_ref[f, b], 5)
        return jnp.where(one == 4, 4, ((one & 1) << 1) + (one >> 1))

    def lateral_code(f, b):
        return lax.rem(link_ref[f, b], 5)

    def ready_vertical(g, carry):
        for f in range(2):
            index = picks(codes(vertical_code, g, (f, f)), row >> 2, slot)
            for c in range(10):
                kghost[g, f, c] = pick(kghost[g, f, c], index)
        return carry

    lax.fori_loop(0, groups, ready_vertical, 0)

    def next_k(x):
        return pltpu.roll(x, LANES - 1, 1)

    def prev_k(x):
        return pltpu.roll(x, 1, 1)

    def next_j(x, edge_x):
        y = pltpu.roll(x, LANES - 16, 1)
        z = pltpu.roll(y, 4, 0)
        if edge_x is not None:
            z = jnp.where(top, z, edge_x)
        return jnp.where(slot == 7, z, y)

    def prev_j(x):
        y = pltpu.roll(x, 16, 1)
        return jnp.where(slot == 0, pltpu.roll(y, 4, 0), y)

    def side(store, n, high):
        order = [(s, t) for s in range(2) for t in range(2)]
        return [store[tuple([*st[:n], high, *st[n:]])] for st in order]

    def children(v, q):
        part = {}
        for a in range(2):
            base = [x + y if a else x - y for x, y in zip(v, q[0])]
            for at, state in enumerate(quads(base, q[1], q[2])):
                part[a, at >> 1, at & 1] = state
        return part, {at: full(state) for at, state in part.items()}

    last_j = (slot == 7) & jnp.logical_not(top)
    zero_j = (slot == 0) & top
    rim_j = last_j | zero_j

    rim_index = jnp.where(top, spot & 7, (spot + 7) & 7) * 16

    def rim_of(i):
        return slot == jnp.where(top, i & 7, (i + 7) & 7)

    def early(g, carry):
        def slopes(i, inner):
            below, above = jnp.maximum(i - 1, 0), jnp.minimum(i + 1, EDGE - 1)
            turn = (i & 7) * 16
            held = rim_of(i)
            for c in range(10):
                x = val[g, c, i]
                at_k = pltpu.roll(kghost[g, 1, c], 15 - i, 1)
                up_k = jnp.where(spot == 15, at_k, next_k(x)) - x
                at_k = pltpu.roll(kghost[g, 0, c], lax.rem(LANES - i, LANES), 1)
                down_k = x - jnp.where(spot == 0, at_k, prev_k(x))
                up_j, down_j = next_j(x, None) - x, x - prev_j(x)
                found = [
                    0.25 * minmod(val[g, c, above] - x, x - val[g, c, below]),
                    0.25 * minmod(up_j, down_j),
                    0.25 * minmod(up_k, down_k),
                ]
                for d in range(3):
                    slope[g, d, c, i] = found[d]
                pltpu.store(cval.at[g, c, i >> 3], pltpu.roll(x, turn, 1), mask=held)
                for d, y in enumerate((found[0], jnp.where(top, up_j, down_j), found[2])):
                    pltpu.store(cslope.at[g, d, c, i >> 3], pltpu.roll(y, turn, 1), mask=held)
                for d, y in enumerate((x - found[2], found[0], found[1])):
                    pltpu.store(first_k.at[g, d, c], pltpu.roll(y, i, 1), mask=spot == i)
            return inner

        lax.fori_loop(0, EDGE, slopes, 0)
        return carry

    lax.fori_loop(0, groups, early, 0)

    def finish(d, carry):
        copy(d).wait()
        return carry

    lax.fori_loop(1, peers, finish, 0)
    mine.wait()
    places.wait()

    def load_lateral(b, carry):
        g, at = b // PACK, lax.rem(b, PACK)
        for f in range(4):
            code = lax.rem(link_ref[f, b], 5)
            base = place_ref[0, b * 4 + f]
            for h in range(2):
                from_row = base + jnp.where(code == 4, h, code >> 1)
                for c in range(10):
                    x = ret_ref[pl.ds(from_row + 2 * c, 1), :]
                    if f < 2:
                        raw_i[g, f, c, pl.ds(h * PACK + at, 1), :] = x
                    else:
                        raw_j[g, c, h, pl.ds((f - 2) * PACK + at, 1), :] = x
        return carry

    lax.fori_loop(0, blocks, load_lateral, 0)

    def group(g, carry):
        for f in range(2):
            index = picks(codes(lateral_code, g, (f, f)), row >> 2, slot)
            for c in range(10):
                raw_i[g, f, c] = pick(raw_i[g, f, c], index)
        code = codes(lateral_code, g, (2, 3))
        for p in range(2):
            index = picks(code, p, jnp.where(top, slot, (slot + 1) & 7))
            for c in range(10):
                raw_j[g, c, p] = pick(raw_j[g, c, p], index)
        for c in range(10):
            for p in range(2):
                own, ghost = cval[g, c, p], raw_j[g, c, p]
                other = jnp.where(top, own - ghost, ghost - own)
                cslope[g, 1, c, p] = 0.25 * minmod(cslope[g, 1, c, p], other)
            first, second = val[g, c, 0], val[g, c, 1]
            x = 0.25 * minmod(second - first, first - raw_i[g, 0, c])
            slope[g, 0, c, 0] = x
            pltpu.store(cslope.at[g, 0, c, 0], x, mask=rim_of(0))
            first, second = val[g, c, EDGE - 2], val[g, c, EDGE - 1]
            x = 0.25 * minmod(raw_i[g, 1, c] - second, second - first)
            slope[g, 0, c, EDGE - 1] = x
            x = pltpu.roll(x, LANES - 16, 1)
            pltpu.store(cslope.at[g, 0, c, 1], x, mask=rim_of(EDGE - 1))

        for c in range(10):
            x = jnp.where(spot == 0, slope[g, 0, c, 0], first_k[g, 1, c])
            first_k[g, 1, c] = jnp.where(spot == 15, pltpu.roll(slope[g, 0, c, EDGE - 1], 15, 1), x)
            parts = [pick(cslope[g, 1, c, p], rim_index) for p in range(2)]
            first_k[g, 2, c] = jnp.where(rim_j, jnp.where(spot < 8, *parts), first_k[g, 2, c])

        for p in range(2):
            for at, x in enumerate(basic([raw_j[g, c, p] for c in range(5)])):
                jedge[at, p] = x
        for at, x in enumerate(basic([kghost[g, 1, c] for c in range(5)])):
            kedge[at] = x
        for at, x in enumerate(basic([raw_i[g, 0, c] for c in range(5)])):
            for s in range(4):
                carry_hi[s, at] = x
        nothing = jnp.zeros((8, LANES), jnp.float32)
        for at in range(3):
            carry_sum[at] = nothing

        def join(at, lefts, rights):
            f = moments(lefts, rights, 0)
            below = jnp.maximum(at - 1, 0)
            outer = [val[g, 5 + c, below] + slope[g, 0, 5 + c, below] for c in range(5)]
            aq1 = [slope[g, 1, 5 + c, below] for c in range(5)]
            aq2 = [slope[g, 2, 5 + c, below] for c in range(5)]
            return f, outer, aq1, aq2

        def layer(i, inner):
            turn = lax.rem(LANES - (i & 7) * 16, LANES)
            compact = i >> 3
            v = [val[g, c, i] for c in range(5)]
            av = [val[g, 5 + c, i] for c in range(5)]
            q = [[slope[g, d, c, i] for c in range(5)] for d in range(3)]
            aq = [[slope[g, d, 5 + c, i] for c in range(5)] for d in range(3)]
            for c in range(5):
                q[1][c] = jnp.where(rim_j, pltpu.roll(cslope[g, 1, c, compact], turn, 1), q[1][c])
                aq[1][c] = jnp.where(rim_j, pltpu.roll(cslope[g, 1, 5 + c, compact], turn, 1), aq[1][c])
                slope[g, 1, 5 + c, i] = aq[1][c]
            part, child = children(v, q)
            own_solid = solid_ref[g, i]
            total = jnp.zeros((8, LANES), jnp.float32)
            wall_above = None
            for n in range(3):
                t1, t2 = [a for a in range(3) if a != n]
                f = [roe(a, b, n) for a, b in zip(side(child, n, 0), side(child, n, 1))]
                inside = [(f[0][c] + f[1][c]) + (f[2][c] + f[3][c]) for c in range(5)]
                total = total - 2.0 * dot(aq[n], inside)
                outer = [x + y for x, y in zip(av, aq[n])]
                inner_side = [x - y for x, y in zip(av, aq[n])]
                cross = aq[t1][1 + n] * q[t1][4] + aq[t2][1 + n] * q[t2][4]
                wall_up = 8.0 * (outer[1 + n] * (v[4] + q[n][4]) + cross)
                wall_down = 8.0 * (inner_side[1 + n] * (v[4] - q[n][4]) + cross)
                if n == 0:
                    lefts = [full([carry_hi[s, at] for at in range(6)]) for s in range(4)]
                    below, before, b1, b2 = join(i, lefts, side(child, 0, 0))
                    for s, state in enumerate(side(part, 0, 1)):
                        for at in range(6):
                            carry_hi[s, at] = state[at]
                    ahead = dot([*before, *b1, *b2], below)
                    total_ref[i] = carry_sum[0] + jnp.where(own_solid > 0.5, carry_sum[1], ahead)
                    lower = dot([*inner_side, *aq[1], *aq[2]], below)
                    total = total - jnp.where(carry_sum[2] > 0.5, wall_down, lower)
                    wall_above = wall_up
                    continue
                if n == 1:
                    rims = [pltpu.roll(jedge[at, i >> 3], turn, 1) for at in range(6)]
                    rights = [
                        full([next_j(x, rim) for x, rim in zip(state, rims)]) for state in side(part, 1, 0)
                    ]
                    above = moments(side(child, 1, 1), rights, 1)
                    below = [prev_j(x) for x in above]
                    up_solid = jnp.where(last_j, 0.0, next_j(own_solid, None))
                    down_solid = prev_j(own_solid)
                    rim = zero_j
                else:
                    rims = [pltpu.roll(kedge[at], 15 - i, 1) for at in range(6)]
                    rights = [
                        full([jnp.where(spot == 15, rim, next_k(x)) for x, rim in zip(state, rims)])
                        for state in side(part, 2, 0)
                    ]
                    above = moments(side(child, 2, 1), rights, 2)
                    below = [prev_k(x) for x in above]
                    up_solid = jnp.where(spot == 15, 0.0, next_k(own_solid))
                    down_solid = prev_k(own_solid)
                    rim = spot == 0
                upper = dot([*outer, *aq[t1], *aq[t2]], above)
                lower = dot([*inner_side, *aq[t1], *aq[t2]], below)
                lower = jnp.where(rim, 0.0, jnp.where(down_solid > 0.5, wall_down, lower))
                total = total + (jnp.where(up_solid > 0.5, wall_up, upper) - lower)
            carry_sum[0] = total
            carry_sum[1] = wall_above
            carry_sum[2] = own_solid
            return inner

        lax.fori_loop(0, EDGE, layer, 0)

        lefts = [full([carry_hi[s, at] for at in range(6)]) for s in range(4)]
        ghost = full(basic([raw_i[g, 1, c] for c in range(5)]))
        below, before, b1, b2 = join(EDGE, lefts, [ghost] * 4)
        total_ref[EDGE] = carry_sum[0] + dot([*before, *b1, *b2], below)

        def start(n, left, x):
            f = moments([full(basic(left))] * 4, [full(s) for s in quads(x[0:5], x[10:15], x[20:25])], n)
            return dot([*x[5:10], *x[15:20], *x[25:30]], f)

        def joined(x):
            return jnp.where(top, x[0], pltpu.roll(x[1], 4, 0))

        low_k = start(2, [kghost[g, 0, c] for c in range(5)], [first_k[g, d, c] for d in range(3) for c in range(10)])
        across = [[joined(cslope[g, d, c]) for c in range(10)] for d in range(3)]
        base = [joined(cval[g, c]) - across[1][c] for c in range(10)]
        found = start(1, [joined(raw_j[g, c]) for c in range(5)], base + across[0] + across[2])
        low_j = [found, pltpu.roll(found, 4, 0)]
        for i in range(EDGE):
            x = total_ref[1 + i] - jnp.where(spot == 0, pltpu.roll(low_k, (LANES - i) % LANES, 1), 0.0)
            x = x - jnp.where(zero_j, pltpu.roll(low_j[i >> 3], (LANES - (i & 7) * 16) % LANES, 1), 0.0)
            found_ref[g, i] = jnp.where(solid_ref[g, i] > 0.5, 0.0, 0.5 * jnp.abs(x))
        return carry

    lax.fori_loop(0, groups, group, 0)

    def write(i, carry):
        for g in range(groups):
            x = found_ref[g, i]
            for h in range(2):
                out_ref[
                    g * PACK : (g + 1) * PACK,
                    pl.ds(pl.multiple_of(i * PLANE + h * LANES, LANES), LANES),
                ] = x[h * PACK : (h + 1) * PACK]
        return carry

    lax.fori_loop(0, EDGE, write, 0)


def local(flow, adjoint, cut_flag, lateral_owner, lateral_link, vertical_link):
    blocks = flow.shape[0]
    groups = blocks // PACK
    peers = lax.axis_size("blk")
    capacity = max(2, 6 * blocks // peers)
    rows = -(-capacity * 20 // 8) * 8
    tile = functools.partial(pltpu.VMEM, dtype=jnp.float32)
    pair = (8, LANES)

    def numbers(space, *shape):
        return space(shape, jnp.int32)

    return pl.pallas_call(
        functools.partial(whole_kernel, capacity),
        out_shape=jax.ShapeDtypeStruct((blocks, EDGE * PLANE), jnp.float32),
        in_specs=[SMEM] * 3 + [HBM] * 3,
        out_specs=VMEM,
        scratch_shapes=[
            tile((5, blocks, EDGE * PLANE)),
            tile((5, blocks, EDGE * PLANE)),
            numbers(pltpu.VMEM, blocks, EDGE * PLANE),
            tile((4, 10, blocks, PLANE)),
            tile((2, 10, blocks, PLANE)),
            numbers(pltpu.VMEM, peers, 1, LANES),
            numbers(pltpu.VMEM, peers, 1, LANES),
            numbers(pltpu.SMEM, peers, 1, LANES),
            numbers(pltpu.VMEM, 1, LANES),
            numbers(pltpu.SMEM, 1, LANES),
            tile((peers, rows, LANES)),
            tile((peers * rows, LANES)),
            tile((10, blocks, PLANE)),
            tile((10, blocks, PLANE)),
            tile((groups, 10, EDGE, *pair)),
            tile((groups, 3, 10, EDGE, *pair)),
            tile((groups, EDGE, *pair)),
            tile((groups, 2, 10, *pair)),
            tile((groups, 10, 2, *pair)),
            tile((groups, 3, 10, 2, *pair)),
            tile((groups, 2, 10, *pair)),
            tile((groups, 10, 2, *pair)),
            tile((6, 2, *pair)),
            tile((6, *pair)),
            tile((4, 6, *pair)),
            tile((3, *pair)),
            tile((groups, 3, 10, *pair)),
            tile((EDGE + 1, *pair)),
            tile((groups, EDGE, *pair)),
            *[pltpu.SemaphoreType.DMA((peers,))] * 4,
            pltpu.SemaphoreType.DMA((2,)),
            pltpu.SemaphoreType.DMA((2,)),
            pltpu.SemaphoreType.DMA,
            pltpu.SemaphoreType.DMA((4,)),
        ],
        compiler_params=pltpu.CompilerParams(
            collective_id=0, has_side_effects=True, vmem_limit_bytes=63 * 1024 * 1024
        ),
        name="indicator",
    )(
        jnp.transpose(lateral_owner, (1, 2, 0)), lateral_link.T, vertical_link.T,
        jnp.transpose(flow, (1, 0, 2)), jnp.transpose(adjoint, (1, 0, 2)), cut_flag,
    )


def solution(mesh):
    spec3 = P(("blk", "grp"), None, None)
    spec2 = P(("blk", "grp"), None)
    return jax.shard_map(
        local,
        mesh=mesh,
        in_specs=(spec3, spec3, spec2, spec3, spec2, spec2),
        out_specs=spec2,
        check_vma=False,
    )
```

```python
import functools

import jax
import jax.numpy as jnp
from jax import lax
from jax.experimental import pallas as pl
from jax.experimental.pallas import tpu as pltpu
from jax.sharding import PartitionSpec as P

EDGE = 16
PLANE = EDGE * EDGE
LANES = 128
PACK = 4
FREESTREAM = (1.0, 0.0, 0.0, 0.3, 1.0)
VMEM = pl.BlockSpec(memory_space=pltpu.VMEM)
SMEM = pl.BlockSpec(memory_space=pltpu.SMEM)
HBM = pl.BlockSpec(memory_space=pltpu.HBM)
MESH = pl.DeviceIdType.MESH


def iota(shape, dim):
    return lax.broadcasted_iota(jnp.int32, shape, dim)


def primitive(state):
    density, mom, energy = state[0], state[1:4], state[4]
    root = lax.rsqrt(density)
    inverse = root * root
    vel = [m * inverse for m in mom]
    square = vel[0] * vel[0] + vel[1] * vel[1] + vel[2] * vel[2]
    return [density, *vel, 0.4 * (energy - 0.5 * density * square)]


def pack_cells(flow_ref, adj_ref, flag_ref, val_ref, solid_ref):
    blocks = flow_ref.shape[1]
    groups = blocks // PACK
    top = iota((8, LANES), 0) < PACK

    def pack(parts):
        tiles = []
        for g in range(groups):
            at = g * PACK % 8
            first, second = parts[g * PACK // 8]
            if first.shape[0] == PACK:
                tiles.append(jnp.concatenate([first, second], axis=0))
            elif at == 0:
                tiles.append(jnp.where(top, first, pltpu.roll(second, 4, 0)))
            else:
                tiles.append(jnp.where(top, pltpu.roll(first, 4, 0), second))
        return tiles

    def read(load, i):
        parts = []
        for start in range(0, blocks, 8):
            rows = slice(start, min(start + 8, blocks))
            parts.append(
                [load(rows, pl.ds(pl.multiple_of(i * PLANE + h * LANES, LANES), LANES)) for h in range(2)]
            )
        return pack(parts)

    def load_layer(i, carry):
        flow = [read(lambda r, s: flow_ref[c, r, s], i) for c in range(5)]
        for g in range(groups):
            for c, x in enumerate(primitive([f[g] for f in flow])):
                val_ref[g, c, i] = x
        for c in range(5):
            for g, x in enumerate(read(lambda r, s: adj_ref[c, r, s], i)):
                val_ref[g, 5 + c, i] = x
        for g, x in enumerate(read(lambda r, s: flag_ref[r, s], i)):
            solid_ref[g, i] = x.astype(jnp.float32)
        return carry

    lax.fori_loop(0, EDGE, load_layer, 0)


def minmod(a, b):
    return jnp.where(a * b > 0.0, jnp.where(jnp.abs(a) < jnp.abs(b), a, b), 0.0)


def basic(state):
    rho, u, v, w, p = state
    inv_root = lax.rsqrt(rho)
    root = rho * inv_root
    enth = (3.5 * p) * (inv_root * inv_root) + 0.5 * (u * u + v * v + w * w)
    return [root, u, v, w, p, enth]


def full(parts):
    root, u, v, w, p, enth = parts
    return (root, (u, v, w), p, enth, (root * u, root * v, root * w), root * enth)


def roe(left, right, n):
    root_l, vel_l, p_l, h_l, rv_l, rh_l = left
    root_r, vel_r, p_r, h_r, rv_r, rh_r = right
    r = lax.rsqrt(root_l + root_r)
    inv = r * r
    vel = [(a + b) * inv for a, b in zip(rv_l, rv_r)]
    enth = (rh_l + rh_r) * inv
    un = vel[n]
    c_sq = 0.4 * enth - 0.2 * (vel[0] * vel[0] + vel[1] * vel[1] + vel[2] * vel[2])
    inv_c = lax.rsqrt(c_sq)
    c = c_sq * inv_c
    speed = jnp.abs(un)
    mach = speed * inv_c
    t = 1.0 - mach
    z = jnp.maximum(0.2 - jnp.abs(t), 0.0)
    w = (1.25 * z) * z
    even = jnp.maximum(t, 0.0) + w
    odd = 1.0 - even
    odd = jnp.where(un < 0.0, -odd, odd)
    dp = p_r - p_l
    a = dp * inv_c
    b = (root_l * root_r) * (vel_r[n] - vel_l[n])
    first = (even * a + odd * b) * inv
    second = c * (odd * a + even * b)
    m_l = root_l * (root_l * (vel_l[n] + speed) - first)
    m_r = root_r * (root_r * (vel_r[n] - speed) - first)
    out = [m_l + m_r] + [m_l * x + m_r * y for x, y in zip(vel_l, vel_r)]
    out[1 + n] = out[1 + n] + ((p_l + p_r) - second)
    out.append((m_l * h_l + m_r * h_r) + (speed * dp - second * un))
    return out


def quads(base, q1, q2):
    low = [b - q for b, q in zip(base, q1)]
    high = [b + q for b, q in zip(base, q1)]
    return [
        basic([b - q for b, q in zip(low, q2)]),
        basic([b + q for b, q in zip(low, q2)]),
        basic([b - q for b, q in zip(high, q2)]),
        basic([b + q for b, q in zip(high, q2)]),
    ]


def moments(lefts, rights, n):
    f = [roe(a, b, n) for a, b in zip(lefts, rights)]
    zero, first, second = [], [], []
    for c in range(5):
        low, high = f[0][c] + f[1][c], f[2][c] + f[3][c]
        zero.append(low + high)
        first.append(high - low)
        second.append((f[1][c] - f[0][c]) + (f[3][c] - f[2][c]))
    return zero + first + second


def dot(a, b):
    total = a[0] * b[0]
    for x, y in zip(a[1:], b[1:]):
        total = total + x * y
    return total


def whole_kernel(
    capacity, owner_ref, link_ref, ver_link_ref, flow_hbm, adj_hbm, flag_hbm, out_ref,
    flow_ref, adj_ref, flag_ref, lat_ref, ver_ref, req_ref, want_ref, index_ref, spot_ref, place_ref,
    stage, ret_ref, low_ref, high_ref,
    val, slope, solid_ref, kghost, cval, cslope,
    raw_i, raw_j, jedge, kedge, carry_hi, carry_sum, first_k, total_ref, found_ref,
    ask_sem, asked_sem, send_sem, recv_sem, up_sem, down_sem, own_sem, in_sem,
):
    blocks = flow_ref.shape[1]
    groups = blocks // PACK
    peers = req_ref.shape[0]
    rows = stage.shape[1]
    used = capacity * 20
    me = lax.axis_index("blk")
    region = lax.axis_index("grp")
    last = lax.axis_size("grp") - 1
    has_low, has_high = region > 0, region < last

    barrier = pltpu.get_barrier_semaphore()
    for d in range(1, peers):
        pl.semaphore_signal(
            barrier, inc=1, device_id={"blk": lax.rem(me + d, peers)}, device_id_type=MESH
        )
    for there, step in ((has_low, -1), (has_high, 1)):
        @pl.when(there)
        def _():
            pl.semaphore_signal(
                barrier, inc=1, device_id={"grp": region + step}, device_id_type=MESH
            )

    loads = [
        pltpu.make_async_copy(a, b, in_sem.at[at])
        for at, (a, b) in enumerate(((flow_hbm, flow_ref), (adj_hbm, adj_ref), (flag_hbm, flag_ref)))
    ]
    for load in loads:
        load.start()

    holder = iota((peers, LANES), 0)
    column = iota((peers, LANES), 1)

    def ask(b, carry):
        asked, count, placed = carry
        for f in range(4):
            code = link_ref[f, b] // 5 * 4 + (f ^ 1)
            match = holder == owner_ref[f, 0, b]
            asked = jnp.where(match & (column == count), code, asked)
            placed = jnp.where(match & (column == b * 4 + f), holder * rows + count * 20, placed)
            count = count + match.astype(jnp.int32)
        return asked, count, placed

    nobody = jnp.zeros((peers, LANES), jnp.int32)
    asked, _, placed = lax.fori_loop(0, blocks, ask, (nobody, nobody, nobody))
    for p in range(peers):
        req_ref[p] = asked[p : p + 1]
    spot_ref[...] = jnp.sum(placed, axis=0, keepdims=True)
    places = pltpu.make_async_copy(spot_ref, place_ref, in_sem.at[3])
    places.start()

    def request(d):
        peer = lax.rem(me + d, peers)
        return pltpu.make_async_remote_copy(
            src_ref=req_ref.at[peer],
            dst_ref=want_ref.at[me],
            send_sem=ask_sem.at[d],
            recv_sem=asked_sem.at[d],
            device_id={"blk": peer},
            device_id_type=MESH,
        )

    own = pltpu.make_async_copy(req_ref.at[me], want_ref.at[me], own_sem)
    own.start()
    lane = iota((blocks, LANES), 1)
    slot, spot = lane >> 4, lane & 15

    def layers(ref, c):
        def tile(i, half):
            return ref[c, :, i * PLANE + half * LANES : i * PLANE + (half + 1) * LANES]

        out = {}
        for half in range(2):
            out[0, half] = tile(0, half)
            out[1, half] = tile(EDGE - 1, half)
            low_j = high_j = low_k = high_k = jnp.zeros((blocks, LANES), jnp.float32)
            for i in range(EDGE):
                if i // 8 == half:
                    il = i % 8
                    low_j = jnp.where(slot == il, pltpu.roll(tile(i, 0), il * 16, 1), low_j)
                    high_j = jnp.where(
                        slot == il, pltpu.roll(tile(i, 1), (il * 16 + 16) % LANES, 1), high_j
                    )
                here = tile(i, half)
                low_k = jnp.where(spot == i, pltpu.roll(here, i, 1), low_k)
                high_k = jnp.where(spot == i, pltpu.roll(here, (LANES + i - 15) % LANES, 1), high_k)
            out[2, half], out[3, half], out[4, half], out[5, half] = low_j, high_j, low_k, high_k
        return out

    def put(face, half, c, value):
        where = slice(half * LANES, (half + 1) * LANES)
        if face < 4:
            lat_ref[face, c, :, where] = value
        else:
            ver_ref[face - 4, c, :, where] = value

    loads[0].wait()
    loads[1].wait()
    def split(c, carry):
        if c == 2:
            pl.semaphore_wait(
                barrier, peers - 1 + has_low.astype(jnp.int32) + has_high.astype(jnp.int32)
            )
            for d in range(1, peers):
                request(d).start()
        for (face, half), value in layers(flow_ref, c).items():
            put(face, half, c, value)
        for (face, half), value in layers(adj_ref, c).items():
            put(face, half, 5 + c, value)
        return carry

    for c in range(5):
        split(c, 0)
    for half in range(2):
        where = slice(half * LANES, (half + 1) * LANES)
        for ref, count in ((ver_ref, 2), (lat_ref, 4)):
            for face in range(count):
                prim = primitive([ref[face, c, :, where] for c in range(5)])
                for c in range(1, 5):
                    ref[face, c, :, where] = prim[c]

    def vertical(source, target, sem, step):
        return pltpu.make_async_remote_copy(
            src_ref=ver_ref.at[source],
            dst_ref=target,
            send_sem=sem.at[0],
            recv_sem=sem.at[1],
            device_id={"grp": region + step},
            device_id_type=MESH,
        )

    upward = vertical(1, low_ref, up_sem, 1)
    downward = vertical(0, high_ref, down_sem, -1)

    @pl.when(has_high)
    def _():
        upward.start()

    @pl.when(has_low)
    def _():
        downward.start()

    loads[2].wait()
    pack_cells(flow_ref, adj_ref, flag_ref, val, solid_ref)

    own.wait()
    for d in range(1, peers):
        request(d).wait()
    indices = pltpu.make_async_copy(want_ref, index_ref, own_sem)
    indices.start()
    indices.wait()

    def copy(d):
        peer = lax.rem(me + d, peers)
        return pltpu.make_async_remote_copy(
            src_ref=stage.at[peer, pl.ds(0, used)],
            dst_ref=ret_ref.at[pl.ds(pl.multiple_of(me * rows, 8), used)],
            send_sem=send_sem.at[d],
            recv_sem=recv_sem.at[d],
            device_id={"blk": peer},
            device_id_type=MESH,
        )

    def gather(peer):
        def one(s, carry):
            code = index_ref[peer, 0, s]
            face, block = code & 3, code >> 2
            for c in range(10):
                x = lat_ref[face, c, pl.ds(block, 1), :]
                for h in range(2):
                    stage[peer, pl.ds(s * 20 + c * 2 + h, 1), :] = x[:, h * LANES : (h + 1) * LANES]
            return carry

        lax.fori_loop(0, capacity, one, 0)

    def send(t, carry):
        sign = 2 * lax.rem(t, 2) - 1
        d = peers // 2 + (t + 1) // 2 * sign
        gather(lax.rem(me + d, peers))
        copy(d).start()
        return carry

    lax.fori_loop(0, peers - 1, send, 0)
    gather(me)
    mine = pltpu.make_async_copy(
        stage.at[me, pl.ds(0, used)], ret_ref.at[pl.ds(pl.multiple_of(me * rows, 8), used)], own_sem
    )
    mine.start()

    def far(ref):
        for c in range(10):
            ref[c] = jnp.full(ref.shape[1:], FREESTREAM[c] if c < 5 else 0.0, jnp.float32)

    @pl.when(has_low)
    def _():
        downward.wait_send()
        upward.wait_recv()

    @pl.when(jnp.logical_not(has_low))
    def _():
        far(low_ref)

    @pl.when(has_high)
    def _():
        upward.wait_send()
        downward.wait_recv()

    @pl.when(jnp.logical_not(has_high))
    def _():
        far(high_ref)

    lane = iota((8, LANES), 1)
    row = iota((8, LANES), 0)
    top = row < PACK
    slot, spot = lane >> 4, lane & 15


    def load_vertical(b, carry):
        g, at = b // PACK, lax.rem(b, PACK)
        for f, ref in enumerate((low_ref, high_ref)):
            link = ver_link_ref[f, b]
            code, block = lax.rem(link, 5), link // 5
            halves = [jnp.where(code == 4, h, code & 1) == 1 for h in range(2)]
            for c in range(10):
                x = ref[c, pl.ds(block, 1), :]
                for h, upper in enumerate(halves):
                    y = jnp.where(upper, x[:, LANES:], x[:, :LANES])
                    kghost[g, f, c, pl.ds(h * PACK + at, 1), :] = y
        return carry

    lax.fori_loop(0, blocks, load_vertical, 0)

    def codes(one_of, g, faces):
        code = jnp.zeros((8, LANES), jnp.int32)
        for r in range(8):
            code = jnp.where(row == r, one_of(faces[r // PACK], g * PACK + r % PACK), code)
        return code

    def picks(code, half, at):
        quarter = ((4 * half + (at >> 1)) << 4) + ((code & 1) << 3) + (spot >> 1)
        return jnp.where(code == 4, at * 16 + spot, quarter)

    def pick(x, index):
        return jnp.take_along_axis(x, index, axis=1, mode="promise_in_bounds")

    def vertical_code(f, b):
        one = lax.rem(ver_link_ref[f, b], 5)
        return jnp.where(one == 4, 4, ((one & 1) << 1) + (one >> 1))

    def lateral_code(f, b):
        return lax.rem(link_ref[f, b], 5)

    def ready_vertical(g, carry):
        for f in range(2):
            index = picks(codes(vertical_code, g, (f, f)), row >> 2, slot)
            for c in range(10):
                kghost[g, f, c] = pick(kghost[g, f, c], index)
        return carry

    lax.fori_loop(0, groups, ready_vertical, 0)

    def next_k(x):
        return pltpu.roll(x, LANES - 1, 1)

    def prev_k(x):
        return pltpu.roll(x, 1, 1)

    def next_j(x, edge_x):
        y = pltpu.roll(x, LANES - 16, 1)
        z = pltpu.roll(y, 4, 0)
        if edge_x is not None:
            z = jnp.where(top, z, edge_x)
        return jnp.where(slot == 7, z, y)

    def prev_j(x):
        y = pltpu.roll(x, 16, 1)
        return jnp.where(slot == 0, pltpu.roll(y, 4, 0), y)

    def side(store, n, high):
        order = [(s, t) for s in range(2) for t in range(2)]
        return [store[tuple([*st[:n], high, *st[n:]])] for st in order]

    def children(v, q):
        part = {}
        for a in range(2):
            base = [x + y if a else x - y for x, y in zip(v, q[0])]
            for at, state in enumerate(quads(base, q[1], q[2])):
                part[a, at >> 1, at & 1] = state
        return part, {at: full(state) for at, state in part.items()}

    last_j = (slot == 7) & jnp.logical_not(top)
    zero_j = (slot == 0) & top
    rim_j = last_j | zero_j

    rim_index = jnp.where(top, spot & 7, (spot + 7) & 7) * 16

    def rim_of(i):
        return slot == jnp.where(top, i & 7, (i + 7) & 7)

    def early(g, carry):
        def slopes(i, inner):
            below, above = jnp.maximum(i - 1, 0), jnp.minimum(i + 1, EDGE - 1)
            turn = (i & 7) * 16
            held = rim_of(i)
            for c in range(10):
                x = val[g, c, i]
                at_k = pltpu.roll(kghost[g, 1, c], 15 - i, 1)
                up_k = jnp.where(spot == 15, at_k, next_k(x)) - x
                at_k = pltpu.roll(kghost[g, 0, c], lax.rem(LANES - i, LANES), 1)
                down_k = x - jnp.where(spot == 0, at_k, prev_k(x))
                up_j, down_j = next_j(x, None) - x, x - prev_j(x)
                found = [
                    0.25 * minmod(val[g, c, above] - x, x - val[g, c, below]),
                    0.25 * minmod(up_j, down_j),
                    0.25 * minmod(up_k, down_k),
                ]
                for d in range(3):
                    slope[g, d, c, i] = found[d]
                pltpu.store(cval.at[g, c, i >> 3], pltpu.roll(x, turn, 1), mask=held)
                for d, y in enumerate((found[0], jnp.where(top, up_j, down_j), found[2])):
                    pltpu.store(cslope.at[g, d, c, i >> 3], pltpu.roll(y, turn, 1), mask=held)
                for d, y in enumerate((x - found[2], found[0], found[1])):
                    pltpu.store(first_k.at[g, d, c], pltpu.roll(y, i, 1), mask=spot == i)
            return inner

        lax.fori_loop(0, EDGE, slopes, 0)
        return carry

    lax.fori_loop(0, groups, early, 0)

    def finish(d, carry):
        copy(d).wait()
        return carry

    lax.fori_loop(1, peers, finish, 0)
    mine.wait()
    places.wait()

    def load_lateral(b, carry):
        g, at = b // PACK, lax.rem(b, PACK)
        for f in range(4):
            code = lax.rem(link_ref[f, b], 5)
            base = place_ref[0, b * 4 + f]
            for h in range(2):
                from_row = base + jnp.where(code == 4, h, code >> 1)
                for c in range(10):
                    x = ret_ref[pl.ds(from_row + 2 * c, 1), :]
                    if f < 2:
                        raw_i[g, f, c, pl.ds(h * PACK + at, 1), :] = x
                    else:
                        raw_j[g, c, h, pl.ds((f - 2) * PACK + at, 1), :] = x
        return carry

    lax.fori_loop(0, blocks, load_lateral, 0)

    def group(g, carry):
        for f in range(2):
            index = picks(codes(lateral_code, g, (f, f)), row >> 2, slot)
            for c in range(10):
                raw_i[g, f, c] = pick(raw_i[g, f, c], index)
        code = codes(lateral_code, g, (2, 3))
        for p in range(2):
            index = picks(code, p, jnp.where(top, slot, (slot + 1) & 7))
            for c in range(10):
                raw_j[g, c, p] = pick(raw_j[g, c, p], index)
        for c in range(10):
            for p in range(2):
                own, ghost = cval[g, c, p], raw_j[g, c, p]
                other = jnp.where(top, own - ghost, ghost - own)
                cslope[g, 1, c, p] = 0.25 * minmod(cslope[g, 1, c, p], other)
            first, second = val[g, c, 0], val[g, c, 1]
            x = 0.25 * minmod(second - first, first - raw_i[g, 0, c])
            slope[g, 0, c, 0] = x
            pltpu.store(cslope.at[g, 0, c, 0], x, mask=rim_of(0))
            first, second = val[g, c, EDGE - 2], val[g, c, EDGE - 1]
            x = 0.25 * minmod(raw_i[g, 1, c] - second, second - first)
            slope[g, 0, c, EDGE - 1] = x
            x = pltpu.roll(x, LANES - 16, 1)
            pltpu.store(cslope.at[g, 0, c, 1], x, mask=rim_of(EDGE - 1))

        for c in range(10):
            x = jnp.where(spot == 0, slope[g, 0, c, 0], first_k[g, 1, c])
            first_k[g, 1, c] = jnp.where(spot == 15, pltpu.roll(slope[g, 0, c, EDGE - 1], 15, 1), x)
            parts = [pick(cslope[g, 1, c, p], rim_index) for p in range(2)]
            first_k[g, 2, c] = jnp.where(rim_j, jnp.where(spot < 8, *parts), first_k[g, 2, c])

        for p in range(2):
            for at, x in enumerate(basic([raw_j[g, c, p] for c in range(5)])):
                jedge[at, p] = x
        for at, x in enumerate(basic([kghost[g, 1, c] for c in range(5)])):
            kedge[at] = x
        for at, x in enumerate(basic([raw_i[g, 0, c] for c in range(5)])):
            for s in range(4):
                carry_hi[s, at] = x
        nothing = jnp.zeros((8, LANES), jnp.float32)
        for at in range(3):
            carry_sum[at] = nothing

        def join(at, lefts, rights):
            f = moments(lefts, rights, 0)
            below = jnp.maximum(at - 1, 0)
            outer = [val[g, 5 + c, below] + slope[g, 0, 5 + c, below] for c in range(5)]
            aq1 = [slope[g, 1, 5 + c, below] for c in range(5)]
            aq2 = [slope[g, 2, 5 + c, below] for c in range(5)]
            return f, outer, aq1, aq2

        def layer(i, inner):
            turn = lax.rem(LANES - (i & 7) * 16, LANES)
            compact = i >> 3
            v = [val[g, c, i] for c in range(5)]
            av = [val[g, 5 + c, i] for c in range(5)]
            q = [[slope[g, d, c, i] for c in range(5)] for d in range(3)]
            aq = [[slope[g, d, 5 + c, i] for c in range(5)] for d in range(3)]
            for c in range(5):
                q[1][c] = jnp.where(rim_j, pltpu.roll(cslope[g, 1, c, compact], turn, 1), q[1][c])
                aq[1][c] = jnp.where(rim_j, pltpu.roll(cslope[g, 1, 5 + c, compact], turn, 1), aq[1][c])
                slope[g, 1, 5 + c, i] = aq[1][c]
            part, child = children(v, q)
            own_solid = solid_ref[g, i]
            total = jnp.zeros((8, LANES), jnp.float32)
            wall_above = None
            for n in range(3):
                t1, t2 = [a for a in range(3) if a != n]
                f = [roe(a, b, n) for a, b in zip(side(child, n, 0), side(child, n, 1))]
                inside = [(f[0][c] + f[1][c]) + (f[2][c] + f[3][c]) for c in range(5)]
                total = total - 2.0 * dot(aq[n], inside)
                outer = [x + y for x, y in zip(av, aq[n])]
                inner_side = [x - y for x, y in zip(av, aq[n])]
                cross = aq[t1][1 + n] * q[t1][4] + aq[t2][1 + n] * q[t2][4]
                wall_up = 8.0 * (outer[1 + n] * (v[4] + q[n][4]) + cross)
                wall_down = 8.0 * (inner_side[1 + n] * (v[4] - q[n][4]) + cross)
                if n == 0:
                    lefts = [full([carry_hi[s, at] for at in range(6)]) for s in range(4)]
                    below, before, b1, b2 = join(i, lefts, side(child, 0, 0))
                    for s, state in enumerate(side(part, 0, 1)):
                        for at in range(6):
                            carry_hi[s, at] = state[at]
                    ahead = dot([*before, *b1, *b2], below)
                    total_ref[i] = carry_sum[0] + jnp.where(own_solid > 0.5, carry_sum[1], ahead)
                    lower = dot([*inner_side, *aq[1], *aq[2]], below)
                    total = total - jnp.where(carry_sum[2] > 0.5, wall_down, lower)
                    wall_above = wall_up
                    continue
                if n == 1:
                    rims = [pltpu.roll(jedge[at, i >> 3], turn, 1) for at in range(6)]
                    rights = [
                        full([next_j(x, rim) for x, rim in zip(state, rims)]) for state in side(part, 1, 0)
                    ]
                    above = moments(side(child, 1, 1), rights, 1)
                    below = [prev_j(x) for x in above]
                    up_solid = jnp.where(last_j, 0.0, next_j(own_solid, None))
                    down_solid = prev_j(own_solid)
                    rim = zero_j
                else:
                    rims = [pltpu.roll(kedge[at], 15 - i, 1) for at in range(6)]
                    rights = [
                        full([jnp.where(spot == 15, rim, next_k(x)) for x, rim in zip(state, rims)])
                        for state in side(part, 2, 0)
                    ]
                    above = moments(side(child, 2, 1), rights, 2)
                    below = [prev_k(x) for x in above]
                    up_solid = jnp.where(spot == 15, 0.0, next_k(own_solid))
                    down_solid = prev_k(own_solid)
                    rim = spot == 0
                upper = dot([*outer, *aq[t1], *aq[t2]], above)
                lower = dot([*inner_side, *aq[t1], *aq[t2]], below)
                lower = jnp.where(rim, 0.0, jnp.where(down_solid > 0.5, wall_down, lower))
                total = total + (jnp.where(up_solid > 0.5, wall_up, upper) - lower)
            carry_sum[0] = total
            carry_sum[1] = wall_above
            carry_sum[2] = own_solid
            return inner

        lax.fori_loop(0, EDGE, layer, 0, unroll=2)

        lefts = [full([carry_hi[s, at] for at in range(6)]) for s in range(4)]
        ghost = full(basic([raw_i[g, 1, c] for c in range(5)]))
        below, before, b1, b2 = join(EDGE, lefts, [ghost] * 4)
        total_ref[EDGE] = carry_sum[0] + dot([*before, *b1, *b2], below)

        def start(n, left, x):
            f = moments([full(basic(left))] * 4, [full(s) for s in quads(x[0:5], x[10:15], x[20:25])], n)
            return dot([*x[5:10], *x[15:20], *x[25:30]], f)

        def joined(x):
            return jnp.where(top, x[0], pltpu.roll(x[1], 4, 0))

        low_k = start(2, [kghost[g, 0, c] for c in range(5)], [first_k[g, d, c] for d in range(3) for c in range(10)])
        across = [[joined(cslope[g, d, c]) for c in range(10)] for d in range(3)]
        base = [joined(cval[g, c]) - across[1][c] for c in range(10)]
        found = start(1, [joined(raw_j[g, c]) for c in range(5)], base + across[0] + across[2])
        low_j = [found, pltpu.roll(found, 4, 0)]
        for i in range(EDGE):
            x = total_ref[1 + i] - jnp.where(spot == 0, pltpu.roll(low_k, (LANES - i) % LANES, 1), 0.0)
            x = x - jnp.where(zero_j, pltpu.roll(low_j[i >> 3], (LANES - (i & 7) * 16) % LANES, 1), 0.0)
            found_ref[g, i] = jnp.where(solid_ref[g, i] > 0.5, 0.0, 0.5 * jnp.abs(x))
        return carry

    lax.fori_loop(0, groups, group, 0)

    def write(i, carry):
        for g in range(groups):
            x = found_ref[g, i]
            for h in range(2):
                out_ref[
                    g * PACK : (g + 1) * PACK,
                    pl.ds(pl.multiple_of(i * PLANE + h * LANES, LANES), LANES),
                ] = x[h * PACK : (h + 1) * PACK]
        return carry

    lax.fori_loop(0, EDGE, write, 0)


def local(flow, adjoint, cut_flag, lateral_owner, lateral_link, vertical_link):
    blocks = flow.shape[0]
    groups = blocks // PACK
    peers = lax.axis_size("blk")
    capacity = max(2, 6 * blocks // peers)
    rows = -(-capacity * 20 // 8) * 8
    tile = functools.partial(pltpu.VMEM, dtype=jnp.float32)
    pair = (8, LANES)

    def numbers(space, *shape):
        return space(shape, jnp.int32)

    return pl.pallas_call(
        functools.partial(whole_kernel, capacity),
        out_shape=jax.ShapeDtypeStruct((blocks, EDGE * PLANE), jnp.float32),
        in_specs=[SMEM] * 3 + [HBM] * 3,
        out_specs=VMEM,
        scratch_shapes=[
            tile((5, blocks, EDGE * PLANE)),
            tile((5, blocks, EDGE * PLANE)),
            numbers(pltpu.VMEM, blocks, EDGE * PLANE),
            tile((4, 10, blocks, PLANE)),
            tile((2, 10, blocks, PLANE)),
            numbers(pltpu.VMEM, peers, 1, LANES),
            numbers(pltpu.VMEM, peers, 1, LANES),
            numbers(pltpu.SMEM, peers, 1, LANES),
            numbers(pltpu.VMEM, 1, LANES),
            numbers(pltpu.SMEM, 1, LANES),
            tile((peers, rows, LANES)),
            tile((peers * rows, LANES)),
            tile((10, blocks, PLANE)),
            tile((10, blocks, PLANE)),
            tile((groups, 10, EDGE, *pair)),
            tile((groups, 3, 10, EDGE, *pair)),
            tile((groups, EDGE, *pair)),
            tile((groups, 2, 10, *pair)),
            tile((groups, 10, 2, *pair)),
            tile((groups, 3, 10, 2, *pair)),
            tile((groups, 2, 10, *pair)),
            tile((groups, 10, 2, *pair)),
            tile((6, 2, *pair)),
            tile((6, *pair)),
            tile((4, 6, *pair)),
            tile((3, *pair)),
            tile((groups, 3, 10, *pair)),
            tile((EDGE + 1, *pair)),
            tile((groups, EDGE, *pair)),
            *[pltpu.SemaphoreType.DMA((peers,))] * 4,
            pltpu.SemaphoreType.DMA((2,)),
            pltpu.SemaphoreType.DMA((2,)),
            pltpu.SemaphoreType.DMA,
            pltpu.SemaphoreType.DMA((4,)),
        ],
        compiler_params=pltpu.CompilerParams(
            collective_id=0, has_side_effects=True, vmem_limit_bytes=63 * 1024 * 1024
        ),
        name="indicator",
    )(
        jnp.transpose(lateral_owner, (1, 2, 0)), lateral_link.T, vertical_link.T,
        jnp.transpose(flow, (1, 0, 2)), jnp.transpose(adjoint, (1, 0, 2)), cut_flag,
    )


def solution(mesh):
    spec3 = P(("blk", "grp"), None, None)
    spec2 = P(("blk", "grp"), None)
    return jax.shard_map(
        local,
        mesh=mesh,
        in_specs=(spec3, spec3, spec2, spec3, spec2, spec2),
        out_specs=spec2,
        check_vma=False,
    )
```

```python
import functools

import jax
import jax.numpy as jnp
from jax import lax
from jax.experimental import pallas as pl
from jax.experimental.pallas import tpu as pltpu
from jax.sharding import PartitionSpec as P

EDGE = 16
PLANE = EDGE * EDGE
LANES = 128
PACK = 4
FREESTREAM = (1.0, 0.0, 0.0, 0.3, 1.0)
VMEM = pl.BlockSpec(memory_space=pltpu.VMEM)
SMEM = pl.BlockSpec(memory_space=pltpu.SMEM)
HBM = pl.BlockSpec(memory_space=pltpu.HBM)
MESH = pl.DeviceIdType.MESH


def iota(shape, dim):
    return lax.broadcasted_iota(jnp.int32, shape, dim)


def primitive(state):
    density, mom, energy = state[0], state[1:4], state[4]
    root = lax.rsqrt(density)
    inverse = root * root
    vel = [m * inverse for m in mom]
    square = vel[0] * vel[0] + vel[1] * vel[1] + vel[2] * vel[2]
    return [density, *vel, 0.4 * (energy - 0.5 * density * square)]


def pack_cells(flow_ref, adj_ref, flag_ref, val_ref, solid_ref):
    blocks = flow_ref.shape[1]
    groups = blocks // PACK
    top = iota((8, LANES), 0) < PACK

    def pack(parts):
        tiles = []
        for g in range(groups):
            at = g * PACK % 8
            first, second = parts[g * PACK // 8]
            if first.shape[0] == PACK:
                tiles.append(jnp.concatenate([first, second], axis=0))
            elif at == 0:
                tiles.append(jnp.where(top, first, pltpu.roll(second, 4, 0)))
            else:
                tiles.append(jnp.where(top, pltpu.roll(first, 4, 0), second))
        return tiles

    def read(load, i):
        parts = []
        for start in range(0, blocks, 8):
            rows = slice(start, min(start + 8, blocks))
            parts.append(
                [load(rows, pl.ds(pl.multiple_of(i * PLANE + h * LANES, LANES), LANES)) for h in range(2)]
            )
        return pack(parts)

    def load_layer(i, carry):
        flow = [read(lambda r, s: flow_ref[c, r, s], i) for c in range(5)]
        for g in range(groups):
            for c, x in enumerate(primitive([f[g] for f in flow])):
                val_ref[g, c, i] = x
        for c in range(5):
            for g, x in enumerate(read(lambda r, s: adj_ref[c, r, s], i)):
                val_ref[g, 5 + c, i] = x
        for g, x in enumerate(read(lambda r, s: flag_ref[r, s], i)):
            solid_ref[g, i] = x.astype(jnp.float32)
        return carry

    lax.fori_loop(0, EDGE, load_layer, 0, unroll=2)


def minmod(a, b):
    return jnp.where(a * b > 0.0, jnp.where(jnp.abs(a) < jnp.abs(b), a, b), 0.0)


def basic(state):
    rho, u, v, w, p = state
    inv_root = lax.rsqrt(rho)
    root = rho * inv_root
    enth = (3.5 * p) * (inv_root * inv_root) + 0.5 * (u * u + v * v + w * w)
    return [root, u, v, w, p, enth]


def full(parts):
    root, u, v, w, p, enth = parts
    return (root, (u, v, w), p, enth, (root * u, root * v, root * w), root * enth)


def roe(left, right, n):
    root_l, vel_l, p_l, h_l, rv_l, rh_l = left
    root_r, vel_r, p_r, h_r, rv_r, rh_r = right
    r = lax.rsqrt(root_l + root_r)
    inv = r * r
    vel = [(a + b) * inv for a, b in zip(rv_l, rv_r)]
    enth = (rh_l + rh_r) * inv
    un = vel[n]
    c_sq = 0.4 * enth - 0.2 * (vel[0] * vel[0] + vel[1] * vel[1] + vel[2] * vel[2])
    inv_c = lax.rsqrt(c_sq)
    c = c_sq * inv_c
    speed = jnp.abs(un)
    mach = speed * inv_c
    t = 1.0 - mach
    z = jnp.maximum(0.2 - jnp.abs(t), 0.0)
    w = (1.25 * z) * z
    even = jnp.maximum(t, 0.0) + w
    odd = 1.0 - even
    odd = jnp.where(un < 0.0, -odd, odd)
    dp = p_r - p_l
    a = dp * inv_c
    b = (root_l * root_r) * (vel_r[n] - vel_l[n])
    first = (even * a + odd * b) * inv
    second = c * (odd * a + even * b)
    m_l = root_l * (root_l * (vel_l[n] + speed) - first)
    m_r = root_r * (root_r * (vel_r[n] - speed) - first)
    out = [m_l + m_r] + [m_l * x + m_r * y for x, y in zip(vel_l, vel_r)]
    out[1 + n] = out[1 + n] + ((p_l + p_r) - second)
    out.append((m_l * h_l + m_r * h_r) + (speed * dp - second * un))
    return out


def quads(base, q1, q2):
    low = [b - q for b, q in zip(base, q1)]
    high = [b + q for b, q in zip(base, q1)]
    return [
        basic([b - q for b, q in zip(low, q2)]),
        basic([b + q for b, q in zip(low, q2)]),
        basic([b - q for b, q in zip(high, q2)]),
        basic([b + q for b, q in zip(high, q2)]),
    ]


def moments(lefts, rights, n):
    f = [roe(a, b, n) for a, b in zip(lefts, rights)]
    zero, first, second = [], [], []
    for c in range(5):
        low, high = f[0][c] + f[1][c], f[2][c] + f[3][c]
        zero.append(low + high)
        first.append(high - low)
        second.append((f[1][c] - f[0][c]) + (f[3][c] - f[2][c]))
    return zero + first + second


def dot(a, b):
    total = a[0] * b[0]
    for x, y in zip(a[1:], b[1:]):
        total = total + x * y
    return total


def whole_kernel(
    capacity, owner_ref, link_ref, ver_link_ref, flow_hbm, adj_hbm, flag_hbm, out_ref,
    flow_ref, adj_ref, flag_ref, lat_ref, ver_ref, req_ref, want_ref, index_ref, spot_ref, place_ref,
    stage, ret_ref, low_ref, high_ref,
    val, slope, solid_ref, kghost, cval, cslope,
    raw_i, raw_j, jedge, kedge, carry_hi, carry_sum, first_k, total_ref, found_ref,
    ask_sem, asked_sem, send_sem, recv_sem, up_sem, down_sem, own_sem, in_sem,
):
    blocks = flow_ref.shape[1]
    groups = blocks // PACK
    peers = req_ref.shape[0]
    rows = stage.shape[1]
    used = capacity * 20
    me = lax.axis_index("blk")
    region = lax.axis_index("grp")
    last = lax.axis_size("grp") - 1
    has_low, has_high = region > 0, region < last

    barrier = pltpu.get_barrier_semaphore()
    for d in range(1, peers):
        pl.semaphore_signal(
            barrier, inc=1, device_id={"blk": lax.rem(me + d, peers)}, device_id_type=MESH
        )
    for there, step in ((has_low, -1), (has_high, 1)):
        @pl.when(there)
        def _():
            pl.semaphore_signal(
                barrier, inc=1, device_id={"grp": region + step}, device_id_type=MESH
            )

    loads = [
        pltpu.make_async_copy(a, b, in_sem.at[at])
        for at, (a, b) in enumerate(((flow_hbm, flow_ref), (adj_hbm, adj_ref), (flag_hbm, flag_ref)))
    ]
    for load in loads:
        load.start()

    holder = iota((peers, LANES), 0)
    column = iota((peers, LANES), 1)

    def ask(b, carry):
        asked, count, placed = carry
        for f in range(4):
            code = link_ref[f, b] // 5 * 4 + (f ^ 1)
            match = holder == owner_ref[f, 0, b]
            asked = jnp.where(match & (column == count), code, asked)
            placed = jnp.where(match & (column == b * 4 + f), holder * rows + count * 20, placed)
            count = count + match.astype(jnp.int32)
        return asked, count, placed

    nobody = jnp.zeros((peers, LANES), jnp.int32)
    asked, _, placed = lax.fori_loop(0, blocks, ask, (nobody, nobody, nobody))
    for p in range(peers):
        req_ref[p] = asked[p : p + 1]
    spot_ref[...] = jnp.sum(placed, axis=0, keepdims=True)
    places = pltpu.make_async_copy(spot_ref, place_ref, in_sem.at[3])
    places.start()

    def request(d):
        peer = lax.rem(me + d, peers)
        return pltpu.make_async_remote_copy(
            src_ref=req_ref.at[peer],
            dst_ref=want_ref.at[me],
            send_sem=ask_sem.at[d],
            recv_sem=asked_sem.at[d],
            device_id={"blk": peer},
            device_id_type=MESH,
        )

    own = pltpu.make_async_copy(req_ref.at[me], want_ref.at[me], own_sem)
    own.start()
    lane = iota((blocks, LANES), 1)
    slot, spot = lane >> 4, lane & 15

    def layers(ref, c):
        def tile(i, half):
            return ref[c, :, i * PLANE + half * LANES : i * PLANE + (half + 1) * LANES]

        out = {}
        for half in range(2):
            out[0, half] = tile(0, half)
            out[1, half] = tile(EDGE - 1, half)
            low_j = high_j = low_k = high_k = jnp.zeros((blocks, LANES), jnp.float32)
            for i in range(EDGE):
                if i // 8 == half:
                    il = i % 8
                    low_j = jnp.where(slot == il, pltpu.roll(tile(i, 0), il * 16, 1), low_j)
                    high_j = jnp.where(
                        slot == il, pltpu.roll(tile(i, 1), (il * 16 + 16) % LANES, 1), high_j
                    )
                here = tile(i, half)
                low_k = jnp.where(spot == i, pltpu.roll(here, i, 1), low_k)
                high_k = jnp.where(spot == i, pltpu.roll(here, (LANES + i - 15) % LANES, 1), high_k)
            out[2, half], out[3, half], out[4, half], out[5, half] = low_j, high_j, low_k, high_k
        return out

    def put(face, half, c, value):
        where = slice(half * LANES, (half + 1) * LANES)
        if face < 4:
            lat_ref[face, c, :, where] = value
        else:
            ver_ref[face - 4, c, :, where] = value

    loads[0].wait()
    loads[1].wait()
    def split(c, carry):
        if c == 2:
            pl.semaphore_wait(
                barrier, peers - 1 + has_low.astype(jnp.int32) + has_high.astype(jnp.int32)
            )
            for d in range(1, peers):
                request(d).start()
        for (face, half), value in layers(flow_ref, c).items():
            put(face, half, c, value)
        for (face, half), value in layers(adj_ref, c).items():
            put(face, half, 5 + c, value)
        return carry

    for c in range(5):
        split(c, 0)
    for half in range(2):
        where = slice(half * LANES, (half + 1) * LANES)
        for ref, count in ((ver_ref, 2), (lat_ref, 4)):
            for face in range(count):
                prim = primitive([ref[face, c, :, where] for c in range(5)])
                for c in range(1, 5):
                    ref[face, c, :, where] = prim[c]

    def vertical(source, target, sem, step):
        return pltpu.make_async_remote_copy(
            src_ref=ver_ref.at[source],
            dst_ref=target,
            send_sem=sem.at[0],
            recv_sem=sem.at[1],
            device_id={"grp": region + step},
            device_id_type=MESH,
        )

    upward = vertical(1, low_ref, up_sem, 1)
    downward = vertical(0, high_ref, down_sem, -1)

    @pl.when(has_high)
    def _():
        upward.start()

    @pl.when(has_low)
    def _():
        downward.start()

    loads[2].wait()
    pack_cells(flow_ref, adj_ref, flag_ref, val, solid_ref)

    own.wait()
    for d in range(1, peers):
        request(d).wait()
    indices = pltpu.make_async_copy(want_ref, index_ref, own_sem)
    indices.start()
    indices.wait()

    def copy(d):
        peer = lax.rem(me + d, peers)
        return pltpu.make_async_remote_copy(
            src_ref=stage.at[peer, pl.ds(0, used)],
            dst_ref=ret_ref.at[pl.ds(pl.multiple_of(me * rows, 8), used)],
            send_sem=send_sem.at[d],
            recv_sem=recv_sem.at[d],
            device_id={"blk": peer},
            device_id_type=MESH,
        )

    def gather(peer):
        def one(s, carry):
            code = index_ref[peer, 0, s]
            face, block = code & 3, code >> 2
            for c in range(10):
                x = lat_ref[face, c, pl.ds(block, 1), :]
                for h in range(2):
                    stage[peer, pl.ds(s * 20 + c * 2 + h, 1), :] = x[:, h * LANES : (h + 1) * LANES]
            return carry

        lax.fori_loop(0, capacity, one, 0, unroll=min(3, capacity))

    def send(t, carry):
        sign = 2 * lax.rem(t, 2) - 1
        d = peers // 2 + (t + 1) // 2 * sign
        gather(lax.rem(me + d, peers))
        copy(d).start()
        return carry

    lax.fori_loop(0, peers - 1, send, 0)
    gather(me)
    mine = pltpu.make_async_copy(
        stage.at[me, pl.ds(0, used)], ret_ref.at[pl.ds(pl.multiple_of(me * rows, 8), used)], own_sem
    )
    mine.start()

    def far(ref):
        for c in range(10):
            ref[c] = jnp.full(ref.shape[1:], FREESTREAM[c] if c < 5 else 0.0, jnp.float32)

    @pl.when(has_low)
    def _():
        downward.wait_send()
        upward.wait_recv()

    @pl.when(jnp.logical_not(has_low))
    def _():
        far(low_ref)

    @pl.when(has_high)
    def _():
        upward.wait_send()
        downward.wait_recv()

    @pl.when(jnp.logical_not(has_high))
    def _():
        far(high_ref)

    lane = iota((8, LANES), 1)
    row = iota((8, LANES), 0)
    top = row < PACK
    slot, spot = lane >> 4, lane & 15


    def load_vertical(b, carry):
        g, at = b // PACK, lax.rem(b, PACK)
        for f, ref in enumerate((low_ref, high_ref)):
            link = ver_link_ref[f, b]
            code, block = lax.rem(link, 5), link // 5
            halves = [jnp.where(code == 4, h, code & 1) == 1 for h in range(2)]
            for c in range(10):
                x = ref[c, pl.ds(block, 1), :]
                for h, upper in enumerate(halves):
                    y = jnp.where(upper, x[:, LANES:], x[:, :LANES])
                    kghost[g, f, c, pl.ds(h * PACK + at, 1), :] = y
        return carry

    lax.fori_loop(0, blocks, load_vertical, 0, unroll=2)

    def codes(one_of, g, faces):
        code = jnp.zeros((8, LANES), jnp.int32)
        for r in range(8):
            code = jnp.where(row == r, one_of(faces[r // PACK], g * PACK + r % PACK), code)
        return code

    def picks(code, half, at):
        quarter = ((4 * half + (at >> 1)) << 4) + ((code & 1) << 3) + (spot >> 1)
        return jnp.where(code == 4, at * 16 + spot, quarter)

    def pick(x, index):
        return jnp.take_along_axis(x, index, axis=1, mode="promise_in_bounds")

    def vertical_code(f, b):
        one = lax.rem(ver_link_ref[f, b], 5)
        return jnp.where(one == 4, 4, ((one & 1) << 1) + (one >> 1))

    def lateral_code(f, b):
        return lax.rem(link_ref[f, b], 5)

    def ready_vertical(g, carry):
        for f in range(2):
            index = picks(codes(vertical_code, g, (f, f)), row >> 2, slot)
            for c in range(10):
                kghost[g, f, c] = pick(kghost[g, f, c], index)
        return carry

    lax.fori_loop(0, groups, ready_vertical, 0)

    def next_k(x):
        return pltpu.roll(x, LANES - 1, 1)

    def prev_k(x):
        return pltpu.roll(x, 1, 1)

    def next_j(x, edge_x):
        y = pltpu.roll(x, LANES - 16, 1)
        z = pltpu.roll(y, 4, 0)
        if edge_x is not None:
            z = jnp.where(top, z, edge_x)
        return jnp.where(slot == 7, z, y)

    def prev_j(x):
        y = pltpu.roll(x, 16, 1)
        return jnp.where(slot == 0, pltpu.roll(y, 4, 0), y)

    def side(store, n, high):
        order = [(s, t) for s in range(2) for t in range(2)]
        return [store[tuple([*st[:n], high, *st[n:]])] for st in order]

    def children(v, q):
        part = {}
        for a in range(2):
            base = [x + y if a else x - y for x, y in zip(v, q[0])]
            for at, state in enumerate(quads(base, q[1], q[2])):
                part[a, at >> 1, at & 1] = state
        return part, {at: full(state) for at, state in part.items()}

    last_j = (slot == 7) & jnp.logical_not(top)
    zero_j = (slot == 0) & top
    rim_j = last_j | zero_j

    rim_index = jnp.where(top, spot & 7, (spot + 7) & 7) * 16

    def rim_of(i):
        return slot == jnp.where(top, i & 7, (i + 7) & 7)

    def early(g, carry):
        def slopes(i, inner):
            below, above = jnp.maximum(i - 1, 0), jnp.minimum(i + 1, EDGE - 1)
            turn = (i & 7) * 16
            held = rim_of(i)
            for c in range(10):
                x = val[g, c, i]
                at_k = pltpu.roll(kghost[g, 1, c], 15 - i, 1)
                up_k = jnp.where(spot == 15, at_k, next_k(x)) - x
                at_k = pltpu.roll(kghost[g, 0, c], lax.rem(LANES - i, LANES), 1)
                down_k = x - jnp.where(spot == 0, at_k, prev_k(x))
                up_j, down_j = next_j(x, None) - x, x - prev_j(x)
                found = [
                    0.25 * minmod(val[g, c, above] - x, x - val[g, c, below]),
                    0.25 * minmod(up_j, down_j),
                    0.25 * minmod(up_k, down_k),
                ]
                for d in range(3):
                    slope[g, d, c, i] = found[d]
                pltpu.store(cval.at[g, c, i >> 3], pltpu.roll(x, turn, 1), mask=held)
                for d, y in enumerate((found[0], jnp.where(top, up_j, down_j), found[2])):
                    pltpu.store(cslope.at[g, d, c, i >> 3], pltpu.roll(y, turn, 1), mask=held)
                for d, y in enumerate((x - found[2], found[0], found[1])):
                    pltpu.store(first_k.at[g, d, c], pltpu.roll(y, i, 1), mask=spot == i)
            return inner

        lax.fori_loop(0, EDGE, slopes, 0)
        return carry

    lax.fori_loop(0, groups, early, 0)

    def finish(d, carry):
        copy(d).wait()
        return carry

    lax.fori_loop(1, peers, finish, 0)
    mine.wait()
    places.wait()

    def load_lateral(b, carry):
        g, at = b // PACK, lax.rem(b, PACK)
        for f in range(4):
            code = lax.rem(link_ref[f, b], 5)
            base = place_ref[0, b * 4 + f]
            for h in range(2):
                from_row = base + jnp.where(code == 4, h, code >> 1)
                for c in range(10):
                    x = ret_ref[pl.ds(from_row + 2 * c, 1), :]
                    if f < 2:
                        raw_i[g, f, c, pl.ds(h * PACK + at, 1), :] = x
                    else:
                        raw_j[g, c, h, pl.ds((f - 2) * PACK + at, 1), :] = x
        return carry

    lax.fori_loop(0, blocks, load_lateral, 0, unroll=2)

    def group(g, carry):
        for f in range(2):
            index = picks(codes(lateral_code, g, (f, f)), row >> 2, slot)
            for c in range(10):
                raw_i[g, f, c] = pick(raw_i[g, f, c], index)
        code = codes(lateral_code, g, (2, 3))
        for p in range(2):
            index = picks(code, p, jnp.where(top, slot, (slot + 1) & 7))
            for c in range(10):
                raw_j[g, c, p] = pick(raw_j[g, c, p], index)
        for c in range(10):
            for p in range(2):
                own, ghost = cval[g, c, p], raw_j[g, c, p]
                other = jnp.where(top, own - ghost, ghost - own)
                cslope[g, 1, c, p] = 0.25 * minmod(cslope[g, 1, c, p], other)
            first, second = val[g, c, 0], val[g, c, 1]
            x = 0.25 * minmod(second - first, first - raw_i[g, 0, c])
            slope[g, 0, c, 0] = x
            pltpu.store(cslope.at[g, 0, c, 0], x, mask=rim_of(0))
            first, second = val[g, c, EDGE - 2], val[g, c, EDGE - 1]
            x = 0.25 * minmod(raw_i[g, 1, c] - second, second - first)
            slope[g, 0, c, EDGE - 1] = x
            x = pltpu.roll(x, LANES - 16, 1)
            pltpu.store(cslope.at[g, 0, c, 1], x, mask=rim_of(EDGE - 1))

        for c in range(10):
            x = jnp.where(spot == 0, slope[g, 0, c, 0], first_k[g, 1, c])
            first_k[g, 1, c] = jnp.where(spot == 15, pltpu.roll(slope[g, 0, c, EDGE - 1], 15, 1), x)
            parts = [pick(cslope[g, 1, c, p], rim_index) for p in range(2)]
            first_k[g, 2, c] = jnp.where(rim_j, jnp.where(spot < 8, *parts), first_k[g, 2, c])

        for p in range(2):
            for at, x in enumerate(basic([raw_j[g, c, p] for c in range(5)])):
                jedge[at, p] = x
        for at, x in enumerate(basic([kghost[g, 1, c] for c in range(5)])):
            kedge[at] = x
        for at, x in enumerate(basic([raw_i[g, 0, c] for c in range(5)])):
            for s in range(4):
                carry_hi[s, at] = x
        nothing = jnp.zeros((8, LANES), jnp.float32)
        for at in range(3):
            carry_sum[at] = nothing

        def join(at, lefts, rights):
            f = moments(lefts, rights, 0)
            below = jnp.maximum(at - 1, 0)
            outer = [val[g, 5 + c, below] + slope[g, 0, 5 + c, below] for c in range(5)]
            aq1 = [slope[g, 1, 5 + c, below] for c in range(5)]
            aq2 = [slope[g, 2, 5 + c, below] for c in range(5)]
            return f, outer, aq1, aq2

        def layer(i, inner):
            turn = lax.rem(LANES - (i & 7) * 16, LANES)
            compact = i >> 3
            v = [val[g, c, i] for c in range(5)]
            av = [val[g, 5 + c, i] for c in range(5)]
            q = [[slope[g, d, c, i] for c in range(5)] for d in range(3)]
            aq = [[slope[g, d, 5 + c, i] for c in range(5)] for d in range(3)]
            for c in range(5):
                q[1][c] = jnp.where(rim_j, pltpu.roll(cslope[g, 1, c, compact], turn, 1), q[1][c])
                aq[1][c] = jnp.where(rim_j, pltpu.roll(cslope[g, 1, 5 + c, compact], turn, 1), aq[1][c])
                slope[g, 1, 5 + c, i] = aq[1][c]
            part, child = children(v, q)
            own_solid = solid_ref[g, i]
            total = jnp.zeros((8, LANES), jnp.float32)
            wall_above = None
            for n in range(3):
                t1, t2 = [a for a in range(3) if a != n]
                f = [roe(a, b, n) for a, b in zip(side(child, n, 0), side(child, n, 1))]
                inside = [(f[0][c] + f[1][c]) + (f[2][c] + f[3][c]) for c in range(5)]
                total = total - 2.0 * dot(aq[n], inside)
                outer = [x + y for x, y in zip(av, aq[n])]
                inner_side = [x - y for x, y in zip(av, aq[n])]
                cross = aq[t1][1 + n] * q[t1][4] + aq[t2][1 + n] * q[t2][4]
                wall_up = 8.0 * (outer[1 + n] * (v[4] + q[n][4]) + cross)
                wall_down = 8.0 * (inner_side[1 + n] * (v[4] - q[n][4]) + cross)
                if n == 0:
                    lefts = [full([carry_hi[s, at] for at in range(6)]) for s in range(4)]
                    below, before, b1, b2 = join(i, lefts, side(child, 0, 0))
                    for s, state in enumerate(side(part, 0, 1)):
                        for at in range(6):
                            carry_hi[s, at] = state[at]
                    ahead = dot([*before, *b1, *b2], below)
                    total_ref[i] = carry_sum[0] + jnp.where(own_solid > 0.5, carry_sum[1], ahead)
                    lower = dot([*inner_side, *aq[1], *aq[2]], below)
                    total = total - jnp.where(carry_sum[2] > 0.5, wall_down, lower)
                    wall_above = wall_up
                    continue
                if n == 1:
                    rims = [pltpu.roll(jedge[at, i >> 3], turn, 1) for at in range(6)]
                    rights = [
                        full([next_j(x, rim) for x, rim in zip(state, rims)]) for state in side(part, 1, 0)
                    ]
                    above = moments(side(child, 1, 1), rights, 1)
                    below = [prev_j(x) for x in above]
                    up_solid = jnp.where(last_j, 0.0, next_j(own_solid, None))
                    down_solid = prev_j(own_solid)
                    rim = zero_j
                else:
                    rims = [pltpu.roll(kedge[at], 15 - i, 1) for at in range(6)]
                    rights = [
                        full([jnp.where(spot == 15, rim, next_k(x)) for x, rim in zip(state, rims)])
                        for state in side(part, 2, 0)
                    ]
                    above = moments(side(child, 2, 1), rights, 2)
                    below = [prev_k(x) for x in above]
                    up_solid = jnp.where(spot == 15, 0.0, next_k(own_solid))
                    down_solid = prev_k(own_solid)
                    rim = spot == 0
                upper = dot([*outer, *aq[t1], *aq[t2]], above)
                lower = dot([*inner_side, *aq[t1], *aq[t2]], below)
                lower = jnp.where(rim, 0.0, jnp.where(down_solid > 0.5, wall_down, lower))
                total = total + (jnp.where(up_solid > 0.5, wall_up, upper) - lower)
            carry_sum[0] = total
            carry_sum[1] = wall_above
            carry_sum[2] = own_solid
            return inner

        lax.fori_loop(0, EDGE, layer, 0, unroll=4)

        lefts = [full([carry_hi[s, at] for at in range(6)]) for s in range(4)]
        ghost = full(basic([raw_i[g, 1, c] for c in range(5)]))
        below, before, b1, b2 = join(EDGE, lefts, [ghost] * 4)
        total_ref[EDGE] = carry_sum[0] + dot([*before, *b1, *b2], below)

        def start(n, left, x):
            f = moments([full(basic(left))] * 4, [full(s) for s in quads(x[0:5], x[10:15], x[20:25])], n)
            return dot([*x[5:10], *x[15:20], *x[25:30]], f)

        def joined(x):
            return jnp.where(top, x[0], pltpu.roll(x[1], 4, 0))

        low_k = start(2, [kghost[g, 0, c] for c in range(5)], [first_k[g, d, c] for d in range(3) for c in range(10)])
        across = [[joined(cslope[g, d, c]) for c in range(10)] for d in range(3)]
        base = [joined(cval[g, c]) - across[1][c] for c in range(10)]
        found = start(1, [joined(raw_j[g, c]) for c in range(5)], base + across[0] + across[2])
        low_j = [found, pltpu.roll(found, 4, 0)]
        for i in range(EDGE):
            x = total_ref[1 + i] - jnp.where(spot == 0, pltpu.roll(low_k, (LANES - i) % LANES, 1), 0.0)
            x = x - jnp.where(zero_j, pltpu.roll(low_j[i >> 3], (LANES - (i & 7) * 16) % LANES, 1), 0.0)
            found_ref[g, i] = jnp.where(solid_ref[g, i] > 0.5, 0.0, 0.5 * jnp.abs(x))
        return carry

    lax.fori_loop(0, groups, group, 0)

    def write(i, carry):
        for g in range(groups):
            x = found_ref[g, i]
            for h in range(2):
                out_ref[
                    g * PACK : (g + 1) * PACK,
                    pl.ds(pl.multiple_of(i * PLANE + h * LANES, LANES), LANES),
                ] = x[h * PACK : (h + 1) * PACK]
        return carry

    lax.fori_loop(0, EDGE, write, 0, unroll=4)


def local(flow, adjoint, cut_flag, lateral_owner, lateral_link, vertical_link):
    blocks = flow.shape[0]
    groups = blocks // PACK
    peers = lax.axis_size("blk")
    capacity = max(2, 6 * blocks // peers)
    rows = -(-capacity * 20 // 8) * 8
    tile = functools.partial(pltpu.VMEM, dtype=jnp.float32)
    pair = (8, LANES)

    def numbers(space, *shape):
        return space(shape, jnp.int32)

    return pl.pallas_call(
        functools.partial(whole_kernel, capacity),
        out_shape=jax.ShapeDtypeStruct((blocks, EDGE * PLANE), jnp.float32),
        in_specs=[SMEM] * 3 + [HBM] * 3,
        out_specs=VMEM,
        scratch_shapes=[
            tile((5, blocks, EDGE * PLANE)),
            tile((5, blocks, EDGE * PLANE)),
            numbers(pltpu.VMEM, blocks, EDGE * PLANE),
            tile((4, 10, blocks, PLANE)),
            tile((2, 10, blocks, PLANE)),
            numbers(pltpu.VMEM, peers, 1, LANES),
            numbers(pltpu.VMEM, peers, 1, LANES),
            numbers(pltpu.SMEM, peers, 1, LANES),
            numbers(pltpu.VMEM, 1, LANES),
            numbers(pltpu.SMEM, 1, LANES),
            tile((peers, rows, LANES)),
            tile((peers * rows, LANES)),
            tile((10, blocks, PLANE)),
            tile((10, blocks, PLANE)),
            tile((groups, 10, EDGE, *pair)),
            tile((groups, 3, 10, EDGE, *pair)),
            tile((groups, EDGE, *pair)),
            tile((groups, 2, 10, *pair)),
            tile((groups, 10, 2, *pair)),
            tile((groups, 3, 10, 2, *pair)),
            tile((groups, 2, 10, *pair)),
            tile((groups, 10, 2, *pair)),
            tile((6, 2, *pair)),
            tile((6, *pair)),
            tile((4, 6, *pair)),
            tile((3, *pair)),
            tile((groups, 3, 10, *pair)),
            tile((EDGE + 1, *pair)),
            tile((groups, EDGE, *pair)),
            *[pltpu.SemaphoreType.DMA((peers,))] * 4,
            pltpu.SemaphoreType.DMA((2,)),
            pltpu.SemaphoreType.DMA((2,)),
            pltpu.SemaphoreType.DMA,
            pltpu.SemaphoreType.DMA((4,)),
        ],
        compiler_params=pltpu.CompilerParams(
            collective_id=0, has_side_effects=True, vmem_limit_bytes=63 * 1024 * 1024
        ),
        name="indicator",
    )(
        jnp.transpose(lateral_owner, (1, 2, 0)), lateral_link.T, vertical_link.T,
        jnp.transpose(flow, (1, 0, 2)), jnp.transpose(adjoint, (1, 0, 2)), cut_flag,
    )


def solution(mesh):
    spec3 = P(("blk", "grp"), None, None)
    spec2 = P(("blk", "grp"), None)
    return jax.shard_map(
        local,
        mesh=mesh,
        in_specs=(spec3, spec3, spec2, spec3, spec2, spec2),
        out_specs=spec2,
        check_vma=False,
    )
```

```python
import functools

import jax
import jax.numpy as jnp
from jax import lax
from jax.experimental import pallas as pl
from jax.experimental.pallas import tpu as pltpu
from jax.sharding import PartitionSpec as P

EDGE = 16
PLANE = EDGE * EDGE
LANES = 128
PACK = 4
FREESTREAM = (1.0, 0.0, 0.0, 0.3, 1.0)
VMEM = pl.BlockSpec(memory_space=pltpu.VMEM)
SMEM = pl.BlockSpec(memory_space=pltpu.SMEM)
HBM = pl.BlockSpec(memory_space=pltpu.HBM)
MESH = pl.DeviceIdType.MESH


def iota(shape, dim):
    return lax.broadcasted_iota(jnp.int32, shape, dim)


def primitive(state):
    density, mom, energy = state[0], state[1:4], state[4]
    root = lax.rsqrt(density)
    inverse = root * root
    vel = [m * inverse for m in mom]
    square = vel[0] * vel[0] + vel[1] * vel[1] + vel[2] * vel[2]
    return [density, *vel, 0.4 * (energy - 0.5 * density * square)]


def pack_cells(flow_ref, adj_ref, flag_ref, val_ref, solid_ref):
    blocks = flow_ref.shape[1]
    groups = blocks // PACK
    top = iota((8, LANES), 0) < PACK

    def pack(parts):
        tiles = []
        for g in range(groups):
            at = g * PACK % 8
            first, second = parts[g * PACK // 8]
            if first.shape[0] == PACK:
                tiles.append(jnp.concatenate([first, second], axis=0))
            elif at == 0:
                tiles.append(jnp.where(top, first, pltpu.roll(second, 4, 0)))
            else:
                tiles.append(jnp.where(top, pltpu.roll(first, 4, 0), second))
        return tiles

    def read(load, i):
        parts = []
        for start in range(0, blocks, 8):
            rows = slice(start, min(start + 8, blocks))
            parts.append(
                [load(rows, pl.ds(pl.multiple_of(i * PLANE + h * LANES, LANES), LANES)) for h in range(2)]
            )
        return pack(parts)

    def load_layer(i, carry):
        flow = [read(lambda r, s: flow_ref[c, r, s], i) for c in range(5)]
        for g in range(groups):
            for c, x in enumerate(primitive([f[g] for f in flow])):
                val_ref[g, c, i] = x
        for c in range(5):
            for g, x in enumerate(read(lambda r, s: adj_ref[c, r, s], i)):
                val_ref[g, 5 + c, i] = x
        for g, x in enumerate(read(lambda r, s: flag_ref[r, s], i)):
            solid_ref[g, i] = x.astype(jnp.float32)
        return carry

    lax.fori_loop(0, EDGE, load_layer, 0, unroll=2)


def minmod(a, b):
    return jnp.where(a * b > 0.0, jnp.where(jnp.abs(a) < jnp.abs(b), a, b), 0.0)


def basic(state):
    rho, u, v, w, p = state
    inv_root = lax.rsqrt(rho)
    root = rho * inv_root
    enth = (3.5 * p) * (inv_root * inv_root) + 0.5 * (u * u + v * v + w * w)
    return [root, u, v, w, p, enth]


def full(parts):
    root, u, v, w, p, enth = parts
    return (root, (u, v, w), p, enth, (root * u, root * v, root * w), root * enth)


def flat(state):
    root, vel, p, enth, rv, rh = state
    return [root, *vel, p, enth, *rv, rh]


def unflat(x):
    return (x[0], tuple(x[1:4]), x[4], x[5], tuple(x[6:9]), x[9])


def roe(left, right, n):
    root_l, vel_l, p_l, h_l, rv_l, rh_l = left
    root_r, vel_r, p_r, h_r, rv_r, rh_r = right
    r = lax.rsqrt(root_l + root_r)
    inv = r * r
    vel = [(a + b) * inv for a, b in zip(rv_l, rv_r)]
    enth = (rh_l + rh_r) * inv
    un = vel[n]
    c_sq = 0.4 * enth - 0.2 * (vel[0] * vel[0] + vel[1] * vel[1] + vel[2] * vel[2])
    inv_c = lax.rsqrt(c_sq)
    c = c_sq * inv_c
    speed = jnp.abs(un)
    mach = speed * inv_c
    t = 1.0 - mach
    z = jnp.maximum(0.2 - jnp.abs(t), 0.0)
    w = (1.25 * z) * z
    even = jnp.maximum(t, 0.0) + w
    odd = 1.0 - even
    odd = jnp.where(un < 0.0, -odd, odd)
    dp = p_r - p_l
    a = dp * inv_c
    b = (root_l * root_r) * (vel_r[n] - vel_l[n])
    first = (even * a + odd * b) * inv
    second = c * (odd * a + even * b)
    m_l = root_l * (root_l * (vel_l[n] + speed) - first)
    m_r = root_r * (root_r * (vel_r[n] - speed) - first)
    out = [m_l + m_r] + [m_l * x + m_r * y for x, y in zip(vel_l, vel_r)]
    out[1 + n] = out[1 + n] + ((p_l + p_r) - second)
    out.append((m_l * h_l + m_r * h_r) + (speed * dp - second * un))
    return out


def quads(base, q1, q2):
    low = [b - q for b, q in zip(base, q1)]
    high = [b + q for b, q in zip(base, q1)]
    return [
        basic([b - q for b, q in zip(low, q2)]),
        basic([b + q for b, q in zip(low, q2)]),
        basic([b - q for b, q in zip(high, q2)]),
        basic([b + q for b, q in zip(high, q2)]),
    ]


def moments(lefts, rights, n):
    f = [roe(a, b, n) for a, b in zip(lefts, rights)]
    zero, first, second = [], [], []
    for c in range(5):
        low, high = f[0][c] + f[1][c], f[2][c] + f[3][c]
        zero.append(low + high)
        first.append(high - low)
        second.append((f[1][c] - f[0][c]) + (f[3][c] - f[2][c]))
    return zero + first + second


def dot(a, b):
    total = a[0] * b[0]
    for x, y in zip(a[1:], b[1:]):
        total = total + x * y
    return total


def whole_kernel(
    capacity, owner_ref, link_ref, ver_link_ref, flow_hbm, adj_hbm, flag_hbm, out_ref,
    flow_ref, adj_ref, flag_ref, lat_ref, ver_ref, req_ref, want_ref, index_ref, spot_ref, place_ref,
    stage, ret_ref, low_ref, high_ref,
    val, slope, solid_ref, kghost, cval, cslope,
    raw_i, raw_j, jedge, kedge, carry_hi, carry_sum, first_k, total_ref, found_ref,
    ask_sem, asked_sem, send_sem, recv_sem, up_sem, down_sem, own_sem, in_sem,
):
    blocks = flow_ref.shape[1]
    groups = blocks // PACK
    peers = req_ref.shape[0]
    rows = stage.shape[1]
    used = capacity * 20
    me = lax.axis_index("blk")
    region = lax.axis_index("grp")
    last = lax.axis_size("grp") - 1
    has_low, has_high = region > 0, region < last

    barrier = pltpu.get_barrier_semaphore()
    for d in range(1, peers):
        pl.semaphore_signal(
            barrier, inc=1, device_id={"blk": lax.rem(me + d, peers)}, device_id_type=MESH
        )
    for there, step in ((has_low, -1), (has_high, 1)):
        @pl.when(there)
        def _():
            pl.semaphore_signal(
                barrier, inc=1, device_id={"grp": region + step}, device_id_type=MESH
            )

    loads = [
        pltpu.make_async_copy(a, b, in_sem.at[at])
        for at, (a, b) in enumerate(((flow_hbm, flow_ref), (adj_hbm, adj_ref), (flag_hbm, flag_ref)))
    ]
    for load in loads:
        load.start()

    holder = iota((peers, LANES), 0)
    column = iota((peers, LANES), 1)

    def ask(b, carry):
        asked, count, placed = carry
        for f in range(4):
            code = link_ref[f, b] // 5 * 4 + (f ^ 1)
            match = holder == owner_ref[f, 0, b]
            asked = jnp.where(match & (column == count), code, asked)
            placed = jnp.where(match & (column == b * 4 + f), holder * rows + count * 20, placed)
            count = count + match.astype(jnp.int32)
        return asked, count, placed

    nobody = jnp.zeros((peers, LANES), jnp.int32)
    asked, _, placed = lax.fori_loop(0, blocks, ask, (nobody, nobody, nobody))
    for p in range(peers):
        req_ref[p] = asked[p : p + 1]
    spot_ref[...] = jnp.sum(placed, axis=0, keepdims=True)
    places = pltpu.make_async_copy(spot_ref, place_ref, in_sem.at[3])
    places.start()

    def request(d):
        peer = lax.rem(me + d, peers)
        return pltpu.make_async_remote_copy(
            src_ref=req_ref.at[peer],
            dst_ref=want_ref.at[me],
            send_sem=ask_sem.at[d],
            recv_sem=asked_sem.at[d],
            device_id={"blk": peer},
            device_id_type=MESH,
        )

    own = pltpu.make_async_copy(req_ref.at[me], want_ref.at[me], own_sem)
    own.start()
    lane = iota((blocks, LANES), 1)
    slot, spot = lane >> 4, lane & 15

    def layers(ref, c):
        def tile(i, half):
            return ref[c, :, i * PLANE + half * LANES : i * PLANE + (half + 1) * LANES]

        out = {}
        for half in range(2):
            out[0, half] = tile(0, half)
            out[1, half] = tile(EDGE - 1, half)
            low_j = high_j = low_k = high_k = jnp.zeros((blocks, LANES), jnp.float32)
            for i in range(EDGE):
                if i // 8 == half:
                    il = i % 8
                    low_j = jnp.where(slot == il, pltpu.roll(tile(i, 0), il * 16, 1), low_j)
                    high_j = jnp.where(
                        slot == il, pltpu.roll(tile(i, 1), (il * 16 + 16) % LANES, 1), high_j
                    )
                here = tile(i, half)
                low_k = jnp.where(spot == i, pltpu.roll(here, i, 1), low_k)
                high_k = jnp.where(spot == i, pltpu.roll(here, (LANES + i - 15) % LANES, 1), high_k)
            out[2, half], out[3, half], out[4, half], out[5, half] = low_j, high_j, low_k, high_k
        return out

    def put(face, half, c, value):
        where = slice(half * LANES, (half + 1) * LANES)
        if face < 4:
            lat_ref[face, c, :, where] = value
        else:
            ver_ref[face - 4, c, :, where] = value

    loads[0].wait()
    loads[1].wait()
    def split(c, carry):
        if c == 2:
            pl.semaphore_wait(
                barrier, peers - 1 + has_low.astype(jnp.int32) + has_high.astype(jnp.int32)
            )
            for d in range(1, peers):
                request(d).start()
        for (face, half), value in layers(flow_ref, c).items():
            put(face, half, c, value)
        for (face, half), value in layers(adj_ref, c).items():
            put(face, half, 5 + c, value)
        return carry

    for c in range(5):
        split(c, 0)
    for half in range(2):
        where = slice(half * LANES, (half + 1) * LANES)
        for ref, count in ((ver_ref, 2), (lat_ref, 4)):
            for face in range(count):
                prim = primitive([ref[face, c, :, where] for c in range(5)])
                for c in range(1, 5):
                    ref[face, c, :, where] = prim[c]

    def vertical(source, target, sem, step):
        return pltpu.make_async_remote_copy(
            src_ref=ver_ref.at[source],
            dst_ref=target,
            send_sem=sem.at[0],
            recv_sem=sem.at[1],
            device_id={"grp": region + step},
            device_id_type=MESH,
        )

    upward = vertical(1, low_ref, up_sem, 1)
    downward = vertical(0, high_ref, down_sem, -1)

    @pl.when(has_high)
    def _():
        upward.start()

    @pl.when(has_low)
    def _():
        downward.start()

    loads[2].wait()
    pack_cells(flow_ref, adj_ref, flag_ref, val, solid_ref)

    own.wait()
    for d in range(1, peers):
        request(d).wait()
    indices = pltpu.make_async_copy(want_ref, index_ref, own_sem)
    indices.start()
    indices.wait()

    def copy(d):
        peer = lax.rem(me + d, peers)
        return pltpu.make_async_remote_copy(
            src_ref=stage.at[peer, pl.ds(0, used)],
            dst_ref=ret_ref.at[pl.ds(pl.multiple_of(me * rows, 8), used)],
            send_sem=send_sem.at[d],
            recv_sem=recv_sem.at[d],
            device_id={"blk": peer},
            device_id_type=MESH,
        )

    def gather(peer):
        def one(s, carry):
            code = index_ref[peer, 0, s]
            face, block = code & 3, code >> 2
            for c in range(10):
                x = lat_ref[face, c, pl.ds(block, 1), :]
                for h in range(2):
                    stage[peer, pl.ds(s * 20 + c * 2 + h, 1), :] = x[:, h * LANES : (h + 1) * LANES]
            return carry

        lax.fori_loop(0, capacity, one, 0, unroll=min(3, capacity))

    def send(t, carry):
        sign = 2 * lax.rem(t, 2) - 1
        d = peers // 2 + (t + 1) // 2 * sign
        gather(lax.rem(me + d, peers))
        copy(d).start()
        return carry

    lax.fori_loop(0, peers - 1, send, 0)
    gather(me)
    mine = pltpu.make_async_copy(
        stage.at[me, pl.ds(0, used)], ret_ref.at[pl.ds(pl.multiple_of(me * rows, 8), used)], own_sem
    )
    mine.start()

    def far(ref):
        for c in range(10):
            ref[c] = jnp.full(ref.shape[1:], FREESTREAM[c] if c < 5 else 0.0, jnp.float32)

    @pl.when(has_low)
    def _():
        downward.wait_send()
        upward.wait_recv()

    @pl.when(jnp.logical_not(has_low))
    def _():
        far(low_ref)

    @pl.when(has_high)
    def _():
        upward.wait_send()
        downward.wait_recv()

    @pl.when(jnp.logical_not(has_high))
    def _():
        far(high_ref)

    lane = iota((8, LANES), 1)
    row = iota((8, LANES), 0)
    top = row < PACK
    slot, spot = lane >> 4, lane & 15


    def load_vertical(b, carry):
        g, at = b // PACK, lax.rem(b, PACK)
        for f, ref in enumerate((low_ref, high_ref)):
            link = ver_link_ref[f, b]
            code, block = lax.rem(link, 5), link // 5
            halves = [jnp.where(code == 4, h, code & 1) == 1 for h in range(2)]
            for c in range(10):
                x = ref[c, pl.ds(block, 1), :]
                for h, upper in enumerate(halves):
                    y = jnp.where(upper, x[:, LANES:], x[:, :LANES])
                    kghost[g, f, c, pl.ds(h * PACK + at, 1), :] = y
        return carry

    lax.fori_loop(0, blocks, load_vertical, 0, unroll=2)

    def codes(one_of, g, faces):
        code = jnp.zeros((8, LANES), jnp.int32)
        for r in range(8):
            code = jnp.where(row == r, one_of(faces[r // PACK], g * PACK + r % PACK), code)
        return code

    def picks(code, half, at):
        quarter = ((4 * half + (at >> 1)) << 4) + ((code & 1) << 3) + (spot >> 1)
        return jnp.where(code == 4, at * 16 + spot, quarter)

    def pick(x, index):
        return jnp.take_along_axis(x, index, axis=1, mode="promise_in_bounds")

    def vertical_code(f, b):
        one = lax.rem(ver_link_ref[f, b], 5)
        return jnp.where(one == 4, 4, ((one & 1) << 1) + (one >> 1))

    def lateral_code(f, b):
        return lax.rem(link_ref[f, b], 5)

    def ready_vertical(g, carry):
        for f in range(2):
            index = picks(codes(vertical_code, g, (f, f)), row >> 2, slot)
            for c in range(10):
                kghost[g, f, c] = pick(kghost[g, f, c], index)
        return carry

    lax.fori_loop(0, groups, ready_vertical, 0)

    def next_k(x):
        return pltpu.roll(x, LANES - 1, 1)

    def prev_k(x):
        return pltpu.roll(x, 1, 1)

    def next_j(x, edge_x):
        y = pltpu.roll(x, LANES - 16, 1)
        z = pltpu.roll(y, 4, 0)
        if edge_x is not None:
            z = jnp.where(top, z, edge_x)
        return jnp.where(slot == 7, z, y)

    def prev_j(x):
        y = pltpu.roll(x, 16, 1)
        return jnp.where(slot == 0, pltpu.roll(y, 4, 0), y)

    def side(store, n, high):
        order = [(s, t) for s in range(2) for t in range(2)]
        return [store[tuple([*st[:n], high, *st[n:]])] for st in order]

    def children(v, q):
        part = {}
        for a in range(2):
            base = [x + y if a else x - y for x, y in zip(v, q[0])]
            for at, state in enumerate(quads(base, q[1], q[2])):
                part[a, at >> 1, at & 1] = state
        return part, {at: full(state) for at, state in part.items()}

    last_j = (slot == 7) & jnp.logical_not(top)
    zero_j = (slot == 0) & top
    rim_j = last_j | zero_j

    rim_index = jnp.where(top, spot & 7, (spot + 7) & 7) * 16

    def rim_of(i):
        return slot == jnp.where(top, i & 7, (i + 7) & 7)

    def early(g, carry):
        def slopes(i, inner):
            below, above = jnp.maximum(i - 1, 0), jnp.minimum(i + 1, EDGE - 1)
            turn = (i & 7) * 16
            held = rim_of(i)
            for c in range(10):
                x = val[g, c, i]
                at_k = pltpu.roll(kghost[g, 1, c], 15 - i, 1)
                up_k = jnp.where(spot == 15, at_k, next_k(x)) - x
                at_k = pltpu.roll(kghost[g, 0, c], lax.rem(LANES - i, LANES), 1)
                down_k = x - jnp.where(spot == 0, at_k, prev_k(x))
                up_j, down_j = next_j(x, None) - x, x - prev_j(x)
                found = [
                    0.25 * minmod(val[g, c, above] - x, x - val[g, c, below]),
                    0.25 * minmod(up_j, down_j),
                    0.25 * minmod(up_k, down_k),
                ]
                for d in range(3):
                    slope[g, d, c, i] = found[d]
                pltpu.store(cval.at[g, c, i >> 3], pltpu.roll(x, turn, 1), mask=held)
                for d, y in enumerate((found[0], jnp.where(top, up_j, down_j), found[2])):
                    pltpu.store(cslope.at[g, d, c, i >> 3], pltpu.roll(y, turn, 1), mask=held)
                for d, y in enumerate((x - found[2], found[0], found[1])):
                    pltpu.store(first_k.at[g, d, c], pltpu.roll(y, i, 1), mask=spot == i)
            return inner

        lax.fori_loop(0, EDGE, slopes, 0)
        return carry

    lax.fori_loop(0, groups, early, 0)

    def finish(d, carry):
        copy(d).wait()
        return carry

    lax.fori_loop(1, peers, finish, 0)
    mine.wait()
    places.wait()

    def load_lateral(b, carry):
        g, at = b // PACK, lax.rem(b, PACK)
        for f in range(4):
            code = lax.rem(link_ref[f, b], 5)
            base = place_ref[0, b * 4 + f]
            for h in range(2):
                from_row = base + jnp.where(code == 4, h, code >> 1)
                for c in range(10):
                    x = ret_ref[pl.ds(from_row + 2 * c, 1), :]
                    if f < 2:
                        raw_i[g, f, c, pl.ds(h * PACK + at, 1), :] = x
                    else:
                        raw_j[g, c, h, pl.ds((f - 2) * PACK + at, 1), :] = x
        return carry

    lax.fori_loop(0, blocks, load_lateral, 0, unroll=2)

    def group(g, carry):
        for f in range(2):
            index = picks(codes(lateral_code, g, (f, f)), row >> 2, slot)
            for c in range(10):
                raw_i[g, f, c] = pick(raw_i[g, f, c], index)
        code = codes(lateral_code, g, (2, 3))
        for p in range(2):
            index = picks(code, p, jnp.where(top, slot, (slot + 1) & 7))
            for c in range(10):
                raw_j[g, c, p] = pick(raw_j[g, c, p], index)
        for c in range(10):
            for p in range(2):
                own, ghost = cval[g, c, p], raw_j[g, c, p]
                other = jnp.where(top, own - ghost, ghost - own)
                cslope[g, 1, c, p] = 0.25 * minmod(cslope[g, 1, c, p], other)
            first, second = val[g, c, 0], val[g, c, 1]
            x = 0.25 * minmod(second - first, first - raw_i[g, 0, c])
            slope[g, 0, c, 0] = x
            pltpu.store(cslope.at[g, 0, c, 0], x, mask=rim_of(0))
            first, second = val[g, c, EDGE - 2], val[g, c, EDGE - 1]
            x = 0.25 * minmod(raw_i[g, 1, c] - second, second - first)
            slope[g, 0, c, EDGE - 1] = x
            x = pltpu.roll(x, LANES - 16, 1)
            pltpu.store(cslope.at[g, 0, c, 1], x, mask=rim_of(EDGE - 1))

        for c in range(10):
            x = jnp.where(spot == 0, slope[g, 0, c, 0], first_k[g, 1, c])
            first_k[g, 1, c] = jnp.where(spot == 15, pltpu.roll(slope[g, 0, c, EDGE - 1], 15, 1), x)
            parts = [pick(cslope[g, 1, c, p], rim_index) for p in range(2)]
            first_k[g, 2, c] = jnp.where(rim_j, jnp.where(spot < 8, *parts), first_k[g, 2, c])

        for p in range(2):
            for at, x in enumerate(basic([raw_j[g, c, p] for c in range(5)])):
                jedge[at, p] = x
        for at, x in enumerate(basic([kghost[g, 1, c] for c in range(5)])):
            kedge[at] = x
        for at, x in enumerate(flat(full(basic([raw_i[g, 0, c] for c in range(5)])))):
            for s in range(4):
                carry_hi[s, at] = x
        nothing = jnp.zeros((8, LANES), jnp.float32)
        for at in range(3):
            carry_sum[at] = nothing

        def join(at, lefts, rights):
            f = moments(lefts, rights, 0)
            below = jnp.maximum(at - 1, 0)
            outer = [val[g, 5 + c, below] + slope[g, 0, 5 + c, below] for c in range(5)]
            aq1 = [slope[g, 1, 5 + c, below] for c in range(5)]
            aq2 = [slope[g, 2, 5 + c, below] for c in range(5)]
            return f, outer, aq1, aq2

        def layer(i, inner):
            turn = lax.rem(LANES - (i & 7) * 16, LANES)
            compact = i >> 3
            v = [val[g, c, i] for c in range(5)]
            av = [val[g, 5 + c, i] for c in range(5)]
            q = [[slope[g, d, c, i] for c in range(5)] for d in range(3)]
            aq = [[slope[g, d, 5 + c, i] for c in range(5)] for d in range(3)]
            for c in range(5):
                q[1][c] = jnp.where(rim_j, pltpu.roll(cslope[g, 1, c, compact], turn, 1), q[1][c])
                aq[1][c] = jnp.where(rim_j, pltpu.roll(cslope[g, 1, 5 + c, compact], turn, 1), aq[1][c])
                slope[g, 1, 5 + c, i] = aq[1][c]
            part, child = children(v, q)
            own_solid = solid_ref[g, i]
            total = jnp.zeros((8, LANES), jnp.float32)
            wall_above = None
            for n in range(3):
                t1, t2 = [a for a in range(3) if a != n]
                f = [roe(a, b, n) for a, b in zip(side(child, n, 0), side(child, n, 1))]
                inside = [(f[0][c] + f[1][c]) + (f[2][c] + f[3][c]) for c in range(5)]
                total = total - 2.0 * dot(aq[n], inside)
                outer = [x + y for x, y in zip(av, aq[n])]
                inner_side = [x - y for x, y in zip(av, aq[n])]
                cross = aq[t1][1 + n] * q[t1][4] + aq[t2][1 + n] * q[t2][4]
                wall_up = 8.0 * (outer[1 + n] * (v[4] + q[n][4]) + cross)
                wall_down = 8.0 * (inner_side[1 + n] * (v[4] - q[n][4]) + cross)
                if n == 0:
                    lefts = [unflat([carry_hi[s, at] for at in range(10)]) for s in range(4)]
                    below, before, b1, b2 = join(i, lefts, side(child, 0, 0))
                    for s, state in enumerate(side(child, 0, 1)):
                        for at, x in enumerate(flat(state)):
                            carry_hi[s, at] = x
                    ahead = dot([*before, *b1, *b2], below)
                    total_ref[i] = carry_sum[0] + jnp.where(own_solid > 0.5, carry_sum[1], ahead)
                    lower = dot([*inner_side, *aq[1], *aq[2]], below)
                    total = total - jnp.where(carry_sum[2] > 0.5, wall_down, lower)
                    wall_above = wall_up
                    continue
                if n == 1:
                    rims = [pltpu.roll(jedge[at, i >> 3], turn, 1) for at in range(6)]
                    rights = [
                        full([next_j(x, rim) for x, rim in zip(state, rims)]) for state in side(part, 1, 0)
                    ]
                    above = moments(side(child, 1, 1), rights, 1)
                    below = [prev_j(x) for x in above]
                    up_solid = jnp.where(last_j, 0.0, next_j(own_solid, None))
                    down_solid = prev_j(own_solid)
                    rim = zero_j
                else:
                    rims = [pltpu.roll(kedge[at], 15 - i, 1) for at in range(6)]
                    rights = [
                        full([jnp.where(spot == 15, rim, next_k(x)) for x, rim in zip(state, rims)])
                        for state in side(part, 2, 0)
                    ]
                    above = moments(side(child, 2, 1), rights, 2)
                    below = [prev_k(x) for x in above]
                    up_solid = jnp.where(spot == 15, 0.0, next_k(own_solid))
                    down_solid = prev_k(own_solid)
                    rim = spot == 0
                upper = dot([*outer, *aq[t1], *aq[t2]], above)
                lower = dot([*inner_side, *aq[t1], *aq[t2]], below)
                lower = jnp.where(rim, 0.0, jnp.where(down_solid > 0.5, wall_down, lower))
                total = total + (jnp.where(up_solid > 0.5, wall_up, upper) - lower)
            carry_sum[0] = total
            carry_sum[1] = wall_above
            carry_sum[2] = own_solid
            return inner

        lax.fori_loop(0, EDGE, layer, 0, unroll=4)

        lefts = [unflat([carry_hi[s, at] for at in range(10)]) for s in range(4)]
        ghost = full(basic([raw_i[g, 1, c] for c in range(5)]))
        below, before, b1, b2 = join(EDGE, lefts, [ghost] * 4)
        total_ref[EDGE] = carry_sum[0] + dot([*before, *b1, *b2], below)

        def start(n, left, x):
            f = moments([full(basic(left))] * 4, [full(s) for s in quads(x[0:5], x[10:15], x[20:25])], n)
            return dot([*x[5:10], *x[15:20], *x[25:30]], f)

        def joined(x):
            return jnp.where(top, x[0], pltpu.roll(x[1], 4, 0))

        low_k = start(2, [kghost[g, 0, c] for c in range(5)], [first_k[g, d, c] for d in range(3) for c in range(10)])
        across = [[joined(cslope[g, d, c]) for c in range(10)] for d in range(3)]
        base = [joined(cval[g, c]) - across[1][c] for c in range(10)]
        found = start(1, [joined(raw_j[g, c]) for c in range(5)], base + across[0] + across[2])
        low_j = [found, pltpu.roll(found, 4, 0)]
        for i in range(EDGE):
            x = total_ref[1 + i] - jnp.where(spot == 0, pltpu.roll(low_k, (LANES - i) % LANES, 1), 0.0)
            x = x - jnp.where(zero_j, pltpu.roll(low_j[i >> 3], (LANES - (i & 7) * 16) % LANES, 1), 0.0)
            found_ref[g, i] = jnp.where(solid_ref[g, i] > 0.5, 0.0, 0.5 * jnp.abs(x))
        return carry

    lax.fori_loop(0, groups, group, 0)

    def write(i, carry):
        for g in range(groups):
            x = found_ref[g, i]
            for h in range(2):
                out_ref[
                    g * PACK : (g + 1) * PACK,
                    pl.ds(pl.multiple_of(i * PLANE + h * LANES, LANES), LANES),
                ] = x[h * PACK : (h + 1) * PACK]
        return carry

    lax.fori_loop(0, EDGE, write, 0, unroll=4)


def local(flow, adjoint, cut_flag, lateral_owner, lateral_link, vertical_link):
    blocks = flow.shape[0]
    groups = blocks // PACK
    peers = lax.axis_size("blk")
    capacity = max(2, 6 * blocks // peers)
    rows = -(-capacity * 20 // 8) * 8
    tile = functools.partial(pltpu.VMEM, dtype=jnp.float32)
    pair = (8, LANES)

    def numbers(space, *shape):
        return space(shape, jnp.int32)

    return pl.pallas_call(
        functools.partial(whole_kernel, capacity),
        out_shape=jax.ShapeDtypeStruct((blocks, EDGE * PLANE), jnp.float32),
        in_specs=[SMEM] * 3 + [HBM] * 3,
        out_specs=VMEM,
        scratch_shapes=[
            tile((5, blocks, EDGE * PLANE)),
            tile((5, blocks, EDGE * PLANE)),
            numbers(pltpu.VMEM, blocks, EDGE * PLANE),
            tile((4, 10, blocks, PLANE)),
            tile((2, 10, blocks, PLANE)),
            numbers(pltpu.VMEM, peers, 1, LANES),
            numbers(pltpu.VMEM, peers, 1, LANES),
            numbers(pltpu.SMEM, peers, 1, LANES),
            numbers(pltpu.VMEM, 1, LANES),
            numbers(pltpu.SMEM, 1, LANES),
            tile((peers, rows, LANES)),
            tile((peers * rows, LANES)),
            tile((10, blocks, PLANE)),
            tile((10, blocks, PLANE)),
            tile((groups, 10, EDGE, *pair)),
            tile((groups, 3, 10, EDGE, *pair)),
            tile((groups, EDGE, *pair)),
            tile((groups, 2, 10, *pair)),
            tile((groups, 10, 2, *pair)),
            tile((groups, 3, 10, 2, *pair)),
            tile((groups, 2, 10, *pair)),
            tile((groups, 10, 2, *pair)),
            tile((6, 2, *pair)),
            tile((6, *pair)),
            tile((4, 10, *pair)),
            tile((3, *pair)),
            tile((groups, 3, 10, *pair)),
            tile((EDGE + 1, *pair)),
            tile((groups, EDGE, *pair)),
            *[pltpu.SemaphoreType.DMA((peers,))] * 4,
            pltpu.SemaphoreType.DMA((2,)),
            pltpu.SemaphoreType.DMA((2,)),
            pltpu.SemaphoreType.DMA,
            pltpu.SemaphoreType.DMA((4,)),
        ],
        compiler_params=pltpu.CompilerParams(
            collective_id=0, has_side_effects=True, vmem_limit_bytes=63 * 1024 * 1024
        ),
        name="indicator",
    )(
        jnp.transpose(lateral_owner, (1, 2, 0)), lateral_link.T, vertical_link.T,
        jnp.transpose(flow, (1, 0, 2)), jnp.transpose(adjoint, (1, 0, 2)), cut_flag,
    )


def solution(mesh):
    spec3 = P(("blk", "grp"), None, None)
    spec2 = P(("blk", "grp"), None)
    return jax.shard_map(
        local,
        mesh=mesh,
        in_specs=(spec3, spec3, spec2, spec3, spec2, spec2),
        out_specs=spec2,
        check_vma=False,
    )
```
